256 devices in a mesh: grid: 8 (over z), dom: 32 (over y, x, core).
Axes of the slice: x: 4, y: 4, z: 8, core: 2. Of those that a mesh axis runs over, the one named last changes fastest.
Arguments:
- nodal_values: float32 [16, 256, 8192], P('grid', None, 'dom'), may hold values from -6 to 6
- source_term: float32 [16, 256, 8192], P('grid', None, 'dom'), may hold values from -6 to 6
- velocity: float32 [16, 2], P('grid'), may hold values from 0.2 to 0.9
- react_rate: float32 [16], P('grid'), may hold values from 0.3 to 3
- levels: int32 [16, 2], P('grid'), may hold values from 5 to 8, as said below
- comb_coefs: int32 [16], P('grid'), may hold values from -1 to 1, as said below
Outputs:
- combined: float32 [16, 256, 8192], P('grid', None, 'dom')
The draws below stay inside these ranges and needn't reach their ends.
Inputs may be any that keep to these rules, and one draw needn't show every extreme that they name: Each grid's two levels sum to 13 or 12. comb_coefs[c] is 1 where the levels of grid c sum to 13 and -1 where they sum to 12.
All inputs are finite; a program needn't handle non-finite values.
Results may differ from the reference program's by a relative error of at most 0.0003.
Values sent between devices are 32-bit elements; how exact they have to be, the bound alone decides.
A program may use at most 64 MiB of HBM per device.

```python
import math
import jax
import jax.numpy as jnp
from jax import lax

MAXL = 8
LINE = 256
LSUM = 13
MINL = 5
CELLS = 8192
COMP = 16
R = 256
N_DOM = 32


def pick_levels(key):
    inner_key = jax.random.fold_in(key, 7)
    first_key, second_key = jax.random.split(inner_key)
    lower_sum = jax.random.randint(first_key, (COMP,), 0, 2)
    level_cols = MINL + jax.random.randint(second_key, (COMP,), 0, 4 - lower_sum)
    level_rows = LSUM - lower_sum - level_cols
    return (lower_sum, level_cols, level_rows)


def draw_levels(key, part):
    lower_sum, level_cols, level_rows = pick_levels(key)
    return jnp.stack([level_cols, level_rows], axis=-1).astype(jnp.int32)


def draw_comb_coefs(key, part):
    lower_sum, level_cols, level_rows = pick_levels(key)
    return (1 - 2 * lower_sum).astype(jnp.int32)


def level_of(key, extent, cuts, smallest, high):
    gain = 1.0
    for dim, blocks in cuts:
        heights = jax.random.uniform(jax.random.fold_in(jax.random.fold_in(key, 6), dim), (blocks,), jnp.float32, smallest / len(cuts), high / len(cuts))
        gain = gain * jnp.repeat(jnp.exp(heights), extent[dim] // blocks).reshape((-1,) + (1,) * (len(extent) - 1 - dim))
    return gain


def bell_draw(key, extent, scale, limit, cuts=(), held_as=jnp.bfloat16):
    loudness = level_of(key, extent, cuts, -0.22, 0.18) if cuts else 1.0
    drawn = jax.random.normal(key, extent, jnp.float32) * scale * loudness
    return jnp.minimum(jnp.maximum(drawn, -limit), limit).astype(held_as)


def setup_inputs(seed: int = 0) -> dict:
    key_list = jax.random.split(jax.random.key(seed), 7)
    return {
        "nodal_values": bell_draw(key_list[0], (COMP, R, CELLS), 1.0, 6.0, ((0, 8), (2, 32)), jnp.float32),
        "source_term": bell_draw(key_list[1], (COMP, R, CELLS), 1.0, 6.0, ((0, 8), (2, 32)), jnp.float32),
        "velocity": jnp.clip(0.2 + 0.7 * jax.random.uniform(key_list[2], (COMP, 2), jnp.float32) ** level_of(key_list[2], (COMP, 2), ((0, 8),), -0.2, 0.2), 0.2, 0.9),
        "react_rate": jnp.clip(jnp.exp(math.log(3.0) - 2.3025851 * jax.random.uniform(key_list[3], (COMP,), jnp.float32) ** level_of(key_list[3], (COMP,), ((0, 8),), -0.2, 0.2)), 0.3, 3.0),
        "levels": draw_levels(jax.random.fold_in(key_list[6], 71), 0),
        "comb_coefs": draw_comb_coefs(jax.random.fold_in(key_list[6], 71), 0),
    }


tau_react = 0.25


def advect_pair(values, ahead, behind, courant):
    return values - 0.5 * courant * (ahead - behind) + 0.5 * courant * courant * (ahead - 2.0 * values + behind)


def grid_layout(level_pair):
    col_count = jnp.left_shift(jnp.int32(1), level_pair[0])
    row_count = jnp.left_shift(jnp.int32(1), level_pair[1])
    block_len = CELLS // N_DOM
    live_count = col_count * row_count // N_DOM
    rows_block = live_count // col_count
    logical = jnp.arange(CELLS, dtype=jnp.int32)
    in_grid = logical < col_count * row_count
    row_num = jnp.where(in_grid, logical // col_count, 0)
    col_num = jnp.where(in_grid, logical % col_count, 0)
    stored_at = (row_num // rows_block) * block_len + (row_num % rows_block) * col_count + col_num
    slot_dev = logical // block_len
    slot_pos = logical % block_len
    slot_live = slot_pos < live_count
    logical_of = jnp.where(slot_live, (slot_dev * rows_block + slot_pos // col_count) * col_count + slot_pos % col_count, 0)
    fine_at = jnp.left_shift(row_num, MAXL - level_pair[1]) * LINE + jnp.left_shift(col_num, MAXL - level_pair[0])
    return {"cols": col_count, "rows": row_count, "inside": in_grid, "rownum": row_num, "colnum": col_num,
            "stored": stored_at, "slotlive": slot_live, "logical": logical_of, "fine": fine_at}


def neighbour(values, position, line_len, offset, compose):
    return jnp.take(values, compose((position + offset + line_len) % line_len), axis=1)


def hierarchize(values, position, line_len, compose):
    spacing = jnp.bitwise_and(position, -position)
    half_w = jnp.where(position > 0, 0.5, 0.0)
    return values - half_w * (neighbour(values, position, line_len, -spacing, compose) + neighbour(values, position, line_len, spacing, compose))


def dehierarchize(values, position, line_len, compose):
    for exponent in range(MAXL - 1, -1, -1):
        spacing = 2 ** exponent
        enabled_flags = jnp.bitwise_and(position, 2 * spacing - 1) == spacing
        lifted = values + 0.5 * (neighbour(values, position, line_len, -spacing, compose) + neighbour(values, position, line_len, spacing, compose))
        values = jnp.where(enabled_flags, lifted, values)
    return values


def advect_along(values, position, line_len, compose, courant):
    return advect_pair(values, neighbour(values, position, line_len, 1, compose), neighbour(values, position, line_len, -1, compose), courant)


def reference(nodal_values, source_term, velocity, react_rate, levels, comb_coefs):
    def first_phase(grid_items):
        grid_vals, grid_src, grid_vel, grid_rate, level_pair = grid_items
        layout = grid_layout(level_pair)
        col_count = layout["cols"]
        row_count = layout["rows"]
        row_num = layout["rownum"]
        col_num = layout["colnum"]
        by_cols = lambda new_pos: row_num * col_count + new_pos
        by_rows = lambda new_pos: new_pos * col_count + col_num
        inside = layout["inside"].astype(jnp.float32)
        values_now = jnp.take(grid_vals, layout["stored"], axis=1) * inside
        forcing = jnp.take(grid_src, layout["stored"], axis=1) * inside
        nu_cols = grid_vel[0] * col_count.astype(jnp.float32) / LINE
        nu_rows = grid_vel[1] * row_count.astype(jnp.float32) / LINE
        values_now = advect_along(values_now, col_num, col_count, by_cols, nu_cols)
        values_now = values_now * (1.0 - tau_react * grid_rate) + tau_react * forcing
        values_now = advect_along(values_now, row_num, row_count, by_rows, nu_rows)
        values_now = hierarchize(values_now, col_num, col_count, by_cols)
        values_now = hierarchize(values_now, row_num, row_count, by_rows)
        return values_now * inside

    surplus_values = lax.map(first_phase, (nodal_values, source_term, velocity, react_rate, levels))

    def add_grid(running, grid_items):
        surplus, level_pair, weight = grid_items
        layout = grid_layout(level_pair)
        running = running.at[:, layout["fine"]].add(weight.astype(jnp.float32) * surplus)
        return running, None

    total_sum, unused = lax.scan(add_grid, jnp.zeros((R, LINE * LINE), jnp.float32), (surplus_values, levels, comb_coefs))

    def second_phase(grid_items):
        grid_vel, level_pair = grid_items
        layout = grid_layout(level_pair)
        col_count = layout["cols"]
        row_count = layout["rows"]
        row_num = layout["rownum"]
        col_num = layout["colnum"]
        by_cols = lambda new_pos: row_num * col_count + new_pos
        by_rows = lambda new_pos: new_pos * col_count + col_num
        inside = layout["inside"].astype(jnp.float32)
        nu_rows = grid_vel[1] * row_count.astype(jnp.float32) / LINE
        values_now = jnp.take(total_sum, layout["fine"], axis=1) * inside
        values_now = dehierarchize(values_now, row_num, row_count, by_rows)
        values_now = advect_along(values_now, row_num, row_count, by_rows, nu_rows)
        values_now = dehierarchize(values_now, col_num, col_count, by_cols)
        values_now = values_now * inside
        return jnp.take(values_now, layout["logical"], axis=1) * layout["slotlive"].astype(jnp.float32)

    return lax.map(second_phase, (velocity, levels))
```

```python
import functools

import jax
import jax.numpy as jnp
from jax import lax
from jax.experimental import pallas as pl
from jax.experimental.pallas import tpu as pltpu
from jax.sharding import PartitionSpec as P

TAU = 0.25
MESH = pl.DeviceIdType.MESH
BLOCKS = {2: (0, 2), 1: (2, 1), 0: (3, 8), 4: (11, 4), 6: (15, 2), 7: (17, 1), 3: (18, 1), 5: (19, 1)}
UP = (2, 1, 0, 4)
DOWN = (0, 4, 6, 7)
UP_ROWS = (0, 120)
DOWN_ROWS = (24, 120)
FIRST_ROWS = (24, 64)
QUARTERS = 4
FAR = 1 << 20
KDIM = 1280


def dot(left, right, dims):
    return lax.dot_general(left, right, (dims, ((), ())), preferred_element_type=jnp.float32)


def split(value):
    high = value.astype(jnp.bfloat16)
    return high, (value - high.astype(jnp.float32)).astype(jnp.bfloat16)


def stencil(courant):
    square = courant * courant
    return 1.0 - square, 0.5 * (square + courant), 0.5 * (square - courant)


def build_tables(grid, step, lv_ref, vel_ref, rate_ref, left_ref, hat_ref):
    lx, m = lv_ref[grid, 0], lv_ref[grid, 1] - 5
    cols = jnp.left_shift(1, lx)
    gap = jnp.left_shift(1, 8 - lx)
    keep = 1.0 - TAU * rate_ref[grid]
    centre, behind, ahead = stencil(vel_ref[grid, 0] * cols.astype(jnp.float32) * (1.0 / 256.0))
    centre, behind, ahead = keep * centre, keep * behind, keep * ahead

    q = lax.broadcasted_iota(jnp.int32, (32, 128), 0) + step * 32
    quarter = jnp.right_shift(q, 6)
    t = q & 63
    row = jnp.right_shift(t, 6 - m)
    j = t & (jnp.right_shift(64, m) - 1)
    place = 64 * quarter + jnp.where(
        j < 8, 8 * j, jnp.where(j < 16, 8 * j - 60, jnp.where(j < 32, 4 * j - 62, 2 * j - 63))
    )
    reach = jnp.where(j < 8, FAR, jnp.where(j < 16, 4, jnp.where(j < 32, 2, 1)))
    slope = jnp.where(j < 8, 0.125, jnp.where(j < 16, 0.25, jnp.where(j < 32, 0.5, 1.0)))
    row_key = jnp.left_shift(jnp.where(j < jnp.right_shift(cols, 2), row, 1 << 12), 8)
    past = 256 - reach + gap
    past = jnp.where(past == 256, 0, past)
    rows = pl.ds(pl.multiple_of(step * 32, 32), 32)
    for half in range(2):
        p = lax.broadcasted_iota(jnp.int32, (1, 128), 1) + 128 * half
        at = jnp.left_shift(p & (cols - 1), 8 - lx)
        key = jnp.left_shift(jnp.right_shift(p, lx), 8)
        other = key ^ row_key
        apart = (at - place) & 255
        delta = apart | other

        def pick(target, weight):
            return jnp.where(delta == target, weight, 0.0)

        here, right, left = delta == 0, delta == reach, delta == 256 - reach
        tree = jnp.where(here, 1.0, 0.0) - jnp.where(right, 0.5, 0.0) - jnp.where(left, 0.5, 0.0)
        full = (
            centre * tree
            + behind * (pick(256 - gap, 1.0) - pick(reach - gap, 0.5) - pick(256 - reach - gap, 0.5))
            + ahead * (pick(gap, 1.0) - pick(reach + gap, 0.5) - pick(past, 0.5))
        )
        high, low = split(full)
        quart = (TAU * tree).astype(jnp.bfloat16)
        for slot, table in enumerate((high, high, low, quart, quart)):
            left_ref[grid, rows, slot * 256 + half * 128 : slot * 256 + half * 128 + 128] = table
        near = jnp.minimum(apart, 256 - apart).astype(jnp.float32)
        hat = jnp.where(other == 0, jnp.maximum(0.0, 1.0 - near * slope), 0.0).astype(jnp.bfloat16)
        lanes = slice(half * 128, half * 128 + 128)
        hat_ref[grid, rows, lanes] = hat
        hat_ref[grid, pl.ds(pl.multiple_of(256 + step * 32, 32), 32), lanes] = hat


def class_weights(grid, lv_ref, vel_ref, scale):
    m = lv_ref[grid, 1] - 5
    rows = jnp.left_shift(1, m).astype(jnp.float32)
    weights = stencil(vel_ref[grid, 1] * rows * 0.125)
    return [[jnp.where(m == c, scale * w, 0.0) for w in weights] for c in range(4)]


class Sums:
    def __init__(self):
        self.held = {}

    def add(self, offset, number, value):
        key = (offset, number)
        self.held[key] = value if key not in self.held else self.held[key] + value


def spread(blocks, weights, own, up, down):
    for c in range(4):
        centre, behind, ahead = weights[c]
        count = 1 << c
        per = 8 >> c
        for n in range(per):
            w = [blocks[k * per + n] for k in range(count)]
            moved = []
            for k in range(count):
                value = centre * w[k]
                if k > 0:
                    value += behind * w[k - 1]
                if k < count - 1:
                    value += ahead * w[k + 1]
                moved.append(value)
            above, below = behind * w[-1], ahead * w[0]
            line = moved + [above]
            own.add(0, n, moved[0])
            up.add(0, n, above)
            if count == 1:
                down.add(0, n, below)
            for k in range(1, count):
                s = k & -k
                own.add(k * 8 // count, n, line[k] - 0.5 * (line[k - s] + line[k + s]))
            level = 2
            while level <= count:
                up.add(8 // level, n, -0.5 * above)
                spill = -0.5 * moved[0]
                if level == count:
                    spill += below
                down.add(8 - 8 // level, n, spill)
                level *= 2


def contribute(chunk, lv_ref, vel_ref, coef_ref, w_ref, total_ref, up_ref, down_ref):
    half, quarter = chunk // QUARTERS, chunk % QUARTERS
    own, up, down = Sums(), Sums(), Sums()
    for grid in range(2):
        weights = class_weights(grid, lv_ref, vel_ref, coef_ref[grid].astype(jnp.float32))
        blocks = [
            w_ref[grid, half, pl.ds(pl.multiple_of(quarter * 64 + 8 * n, 8), 8), :] for n in range(8)
        ]
        spread(blocks, weights, own, up, down)
    for offset, (start, count) in BLOCKS.items():
        for n in range(count):
            at = 8 * (start + n)
            total_ref[chunk, at : at + 8, :] = own.held[offset, n]
            if offset in UP:
                up_ref[chunk, at - UP_ROWS[0] : at - UP_ROWS[0] + 8, :] = up.held[offset, n]
            if offset in DOWN:
                down_ref[chunk, at - DOWN_ROWS[0] : at - DOWN_ROWS[0] + 8, :] = down.held[offset, n]


def interpolate(chunk, lv_ref, vel_ref, all_ref, prev_ref, next_ref, g_ref):
    half, quarter = chunk // QUARTERS, chunk % QUARTERS

    def held(offset, n):
        at = 8 * (BLOCKS[offset][0] + n)
        return all_ref[chunk, at : at + 8, :]

    def before(offset, n):
        at = 8 * (BLOCKS[offset][0] + n) - DOWN_ROWS[0]
        return prev_ref[chunk, at : at + 8, :]

    weights = [class_weights(grid, lv_ref, vel_ref, 1.0) for grid in range(2)]
    sums = [Sums(), Sums()]
    for n in range(8):
        node = {0: held(0, n), 8: next_ref[chunk, 8 * n : 8 * n + 8, :]}
        back = {1: before(0, n)}
        last = back[1]
        for c in range(1, 4):
            if n >= 8 >> c:
                break
            s = 8 >> c
            for k in range(1, 1 << c, 2):
                node[k * s] = held(k * s, n) + 0.5 * (node[k * s - s] + node[k * s + s])
            last = before(8 - s, n) + 0.5 * (last + node[0])
            back[1 << c] = last
        for c in range(4):
            per = 8 >> c
            if n >= per:
                break
            count = 1 << c
            line = [back[count]] + [node[k * per] for k in range(count + 1)]
            for k in range(count):
                for grid in range(2):
                    centre, behind, ahead = weights[grid][c]
                    sums[grid].add(
                        0, k * per + n, centre * line[k + 1] + behind * line[k] + ahead * line[k + 2]
                    )
    for grid in range(2):
        for n in range(8):
            at = pl.ds(pl.multiple_of(quarter * 64 + 8 * n, 8), 8)
            g_ref[grid, half, at, :] = sums[grid].held[0, n]


def kernel(
    nz, nd,
    lv_ref, vel_ref, rate_ref, coef_ref, v_hbm, s_hbm, out_hbm,
    v_ref, s_ref, left_ref, right_ref, hat_ref, w_ref,
    total_ref, up_ref, down_ref, up_in, down_in, minus_in, plus_in,
    all_ref, prev_ref, next_ref, g_ref, out_ref,
    load_sem, store_sem, up_sem, down_sem, minus_sem, plus_sem, gminus_sem, gplus_sem, prev_sem, next_sem,
):
    z, d = lax.axis_index("grid"), lax.axis_index("dom")
    north, south = (lax.rem(z + 1, nz), d), (lax.rem(z + nz - 1, nz), d)
    after, ahead_of = (z, lax.rem(d + 1, nd)), (z, lax.rem(d + nd - 1, nd))
    loads = []
    for grid in range(2):
        for n, (source, target) in enumerate(((v_hbm, v_ref), (s_hbm, s_ref))):
            loads.append(pltpu.make_async_copy(source.at[grid], target.at[grid], load_sem.at[grid, n]))
            loads[-1].start()

    barrier = pltpu.get_barrier_semaphore()
    for peer in (north, south, after, ahead_of):
        pl.semaphore_signal(barrier, inc=1, device_id=peer, device_id_type=MESH)

    def remote(source, target, sems, slot, peer):
        return pltpu.make_async_remote_copy(
            src_ref=source, dst_ref=target, send_sem=sems.at[0, slot], recv_sem=sems.at[1, slot],
            device_id=peer, device_id_type=MESH,
        )

    for grid in range(2):
        @pl.loop(0, 8)
        def _(step):
            build_tables(grid, step, lv_ref, vel_ref, rate_ref, left_ref, hat_ref)

    for grid in range(2):
        loads[2 * grid].wait()
        loads[2 * grid + 1].wait()
        vh, vl = split(v_ref[grid])
        sh, sl = split(s_ref[grid])
        for slot, part in enumerate((vh, vl, vh, sh, sl)):
            right_ref[grid, :, slot * 256 : slot * 256 + 256] = part
        w = dot(left_ref[grid], right_ref[grid], ((1,), (1,)))
        w_ref[grid, 0] = w[:, :128]
        w_ref[grid, 1] = w[:, 128:]

    pl.semaphore_wait(barrier, 4)

    def up_copy(chunk):
        return remote(up_ref.at[chunk], up_in.at[chunk], up_sem, chunk, after)

    def down_copy(chunk):
        return remote(down_ref.at[chunk], down_in.at[chunk], down_sem, chunk, ahead_of)

    far = nz // 2

    @pl.loop(0, nz)
    def _(i):
        off = jnp.where(i % 2 == 0, nz - far + i // 2, far - 1 - (i - 1) // 2)
        chunk = lax.rem(z + off, nz)
        contribute(chunk, lv_ref, vel_ref, coef_ref, w_ref, total_ref, up_ref, down_ref)
        up_copy(chunk).start()
        down_copy(chunk).start()

    def gather_in(chunk, *others):
        up_copy(chunk).wait_recv()
        down_copy(chunk).wait_recv()
        u, w, x = UP_ROWS[1], DOWN_ROWS[0], DOWN_ROWS[0] + DOWN_ROWS[1]
        parts = [o[...] for o in others]

        def at(low, high, value):
            for o in others:
                value = value + o[low:high, :]
            return value

        total_ref[chunk, 0:w, :] = at(0, w, total_ref[chunk, 0:w, :] + up_in[chunk, 0:w, :])
        total_ref[chunk, w:u, :] = at(
            w, u, total_ref[chunk, w:u, :] + up_in[chunk, w:u, :] + down_in[chunk, 0 : u - w, :]
        )
        total_ref[chunk, u:x, :] = at(u, x, total_ref[chunk, u:x, :] + down_in[chunk, u - w : x - w, :])
        if others:
            total_ref[chunk, x:160, :] = at(x, 160, total_ref[chunk, x:160, :])

    def minus_copy(chunk, t):
        return remote(total_ref.at[chunk], minus_in.at[t], minus_sem, t, south)

    def plus_copy(chunk, t):
        return remote(total_ref.at[chunk], plus_in.at[t], plus_sem, t, north)

    for t in range(far):
        chunk = lax.rem(z + nz - far + t, nz)
        if t == 0:
            gather_in(chunk)
        else:
            minus_copy(chunk, t - 1).wait_recv()
            gather_in(chunk, minus_in.at[t - 1])
        minus_copy(chunk, t).start()
        if t < far - 1:
            chunk = lax.rem(z + far - 1 - t, nz)
            if t == 0:
                gather_in(chunk)
            else:
                plus_copy(chunk, t - 1).wait_recv()
                gather_in(chunk, plus_in.at[t - 1])
            plus_copy(chunk, t).start()
    minus_copy(z, far - 1).wait_recv()
    plus_copy(z, far - 2).wait_recv()
    gather_in(z, minus_in.at[far - 1], plus_in.at[far - 2])

    def prev_copy(chunk, source):
        return remote(
            source.at[chunk, DOWN_ROWS[0] : DOWN_ROWS[0] + DOWN_ROWS[1], :], prev_ref.at[chunk], prev_sem, chunk, after
        )

    def next_copy(chunk, source):
        return remote(
            source.at[chunk, FIRST_ROWS[0] : FIRST_ROWS[0] + FIRST_ROWS[1], :], next_ref.at[chunk], next_sem, chunk,
            ahead_of,
        )

    def gminus_copy(chunk, t, source):
        return remote(source.at[chunk], all_ref.at[chunk], gminus_sem, t, south)

    def gplus_copy(chunk, t, source):
        return remote(source.at[chunk], all_ref.at[chunk], gplus_sem, t, north)

    gminus_copy(z, 0, total_ref).start()
    gplus_copy(z, 0, total_ref).start()
    prev_copy(z, total_ref).start()
    next_copy(z, total_ref).start()
    all_ref[z] = total_ref[z]
    for t in range(1, far + 1):
        chunk = lax.rem(z + t, nz)
        gminus_copy(chunk, t - 1, all_ref).wait_recv()
        if t < far:
            gminus_copy(chunk, t, all_ref).start()
        prev_copy(chunk, all_ref).start()
        next_copy(chunk, all_ref).start()
        if t < far:
            chunk = lax.rem(z + nz - t, nz)
            gplus_copy(chunk, t - 1, all_ref).wait_recv()
            if t < far - 1:
                gplus_copy(chunk, t, all_ref).start()
            prev_copy(chunk, all_ref).start()
            next_copy(chunk, all_ref).start()

    @pl.loop(0, nz)
    def _(i):
        off = jnp.where(i % 2 == 0, nz - i // 2, (i + 1) // 2)
        chunk = lax.rem(z + off, nz)
        prev_copy(chunk, all_ref).wait_recv()
        next_copy(chunk, all_ref).wait_recv()
        interpolate(chunk, lv_ref, vel_ref, all_ref, prev_ref, next_ref, g_ref)

    stores = []
    for half in range(2):
        for grid in range(2):
            turned = jnp.transpose(g_ref[grid, half])
            high, low = split(turned)
            lanes = jnp.concatenate([high, low], axis=1)
            out_ref[grid, half * 128 : half * 128 + 128, :] = dot(lanes, hat_ref[grid], ((1,), (0,)))
            rows = slice(half * 128, half * 128 + 128)
            stores.append(
                pltpu.make_async_copy(
                    out_ref.at[grid, rows, :], out_hbm.at[grid, rows, :], store_sem.at[grid, half]
                )
            )
            stores[-1].start()

    @pl.loop(0, nz)
    def _(chunk):
        up_copy(chunk).wait_send()
        down_copy(chunk).wait_send()
        prev_copy(chunk, all_ref).wait_send()
        next_copy(chunk, all_ref).wait_send()

    for t in range(far):
        minus_copy(0, t).wait_send()
        gminus_copy(0, t, all_ref).wait_send()
        if t < far - 1:
            plus_copy(0, t).wait_send()
            gplus_copy(0, t, all_ref).wait_send()
    for store in stores:
        store.wait()


def local(nz, nd, nodal_values, source_term, velocity, react_rate, levels, comb_coefs):
    far = nz // 2
    f32, bf16 = jnp.float32, jnp.bfloat16
    smem = pl.BlockSpec(memory_space=pltpu.SMEM)
    hbm = pl.BlockSpec(memory_space=pl.ANY)
    sem = pltpu.SemaphoreType.DMA
    return pl.pallas_call(
        functools.partial(kernel, nz, nd),
        out_shape=jax.ShapeDtypeStruct((2, 256, 256), f32),
        in_specs=[smem, smem, smem, smem, hbm, hbm],
        out_specs=hbm,
        scratch_shapes=[
            pltpu.VMEM((2, 256, 256), f32),
            pltpu.VMEM((2, 256, 256), f32),
            pltpu.VMEM((2, 256, KDIM), bf16),
            pltpu.VMEM((2, 256, KDIM), bf16),
            pltpu.VMEM((2, 512, 256), bf16),
            pltpu.VMEM((2, 2, 256, 128), f32),
            pltpu.VMEM((nz, 160, 128), f32),
            pltpu.VMEM((nz, 120, 128), f32),
            pltpu.VMEM((nz, 120, 128), f32),
            pltpu.VMEM((nz, 120, 128), f32),
            pltpu.VMEM((nz, 120, 128), f32),
            pltpu.VMEM((far, 160, 128), f32),
            pltpu.VMEM((far - 1, 160, 128), f32),
            pltpu.VMEM((nz, 160, 128), f32),
            pltpu.VMEM((nz, 120, 128), f32),
            pltpu.VMEM((nz, 64, 128), f32),
            pltpu.VMEM((2, 2, 256, 128), f32),
            pltpu.VMEM((2, 256, 256), f32),
            sem((2, 2)),
            sem((2, 2)),
            sem((2, nz)),
            sem((2, nz)),
            sem((2, far)),
            sem((2, far)),
            sem((2, far)),
            sem((2, far)),
            sem((2, nz)),
            sem((2, nz)),
        ],
        compiler_params=pltpu.CompilerParams(collective_id=0, has_side_effects=True, vmem_limit_bytes=32 << 20),
    )(levels, velocity, react_rate, comb_coefs, nodal_values, source_term)


def solution(mesh):
    in_specs = (
        P("grid", None, "dom"),
        P("grid", None, "dom"),
        P("grid", None),
        P("grid"),
        P("grid", None),
        P("grid"),
    )
    body = functools.partial(local, mesh.shape["grid"], mesh.shape["dom"])
    return jax.shard_map(body, mesh=mesh, in_specs=in_specs, out_specs=P("grid", None, "dom"), check_vma=False)
```

```python
import functools

import jax
import jax.numpy as jnp
from jax import lax
from jax.experimental import pallas as pl
from jax.experimental.pallas import tpu as pltpu
from jax.sharding import PartitionSpec as P

TAU = 0.25
MESH = pl.DeviceIdType.MESH
BLOCKS = {2: (0, 2), 1: (2, 1), 0: (3, 8), 4: (11, 4), 6: (15, 2), 7: (17, 1), 3: (18, 1), 5: (19, 1)}
UP = (2, 1, 0, 4)
DOWN = (0, 4, 6, 7)
UP_ROWS = (0, 120)
DOWN_ROWS = (24, 120)
FIRST_ROWS = (24, 64)
QUARTERS = 4
FAR = 1 << 20
KDIM = 1280


def dot(left, right, dims):
    return lax.dot_general(left, right, (dims, ((), ())), preferred_element_type=jnp.float32)


def split(value):
    high = value.astype(jnp.bfloat16)
    return high, (value - high.astype(jnp.float32)).astype(jnp.bfloat16)


def stencil(courant):
    square = courant * courant
    return 1.0 - square, 0.5 * (square + courant), 0.5 * (square - courant)


def build_tables(grid, step, lv_ref, vel_ref, rate_ref, left_ref, hat_ref):
    lx, m = lv_ref[grid, 0], lv_ref[grid, 1] - 5
    cols = jnp.left_shift(1, lx)
    gap = jnp.left_shift(1, 8 - lx)
    keep = 1.0 - TAU * rate_ref[grid]
    centre, behind, ahead = stencil(vel_ref[grid, 0] * cols.astype(jnp.float32) * (1.0 / 256.0))
    centre, behind, ahead = keep * centre, keep * behind, keep * ahead

    q = lax.broadcasted_iota(jnp.int32, (32, 128), 0) + step * 32
    quarter = jnp.right_shift(q, 6)
    t = q & 63
    row = jnp.right_shift(t, 6 - m)
    j = t & (jnp.right_shift(64, m) - 1)
    place = 64 * quarter + jnp.where(
        j < 8, 8 * j, jnp.where(j < 16, 8 * j - 60, jnp.where(j < 32, 4 * j - 62, 2 * j - 63))
    )
    reach = jnp.where(j < 8, FAR, jnp.where(j < 16, 4, jnp.where(j < 32, 2, 1)))
    slope = jnp.where(j < 8, 0.125, jnp.where(j < 16, 0.25, jnp.where(j < 32, 0.5, 1.0)))
    row_key = jnp.left_shift(jnp.where(j < jnp.right_shift(cols, 2), row, 1 << 12), 8)
    past = 256 - reach + gap
    past = jnp.where(past == 256, 0, past)
    rows = pl.ds(pl.multiple_of(step * 32, 32), 32)
    for half in range(2):
        p = lax.broadcasted_iota(jnp.int32, (1, 128), 1) + 128 * half
        at = jnp.left_shift(p & (cols - 1), 8 - lx)
        key = jnp.left_shift(jnp.right_shift(p, lx), 8)
        other = key ^ row_key
        apart = (at - place) & 255
        delta = apart | other

        def pick(target, weight):
            return jnp.where(delta == target, weight, 0.0)

        here, right, left = delta == 0, delta == reach, delta == 256 - reach
        tree = jnp.where(here, 1.0, 0.0) - jnp.where(right, 0.5, 0.0) - jnp.where(left, 0.5, 0.0)
        full = (
            centre * tree
            + behind * (pick(256 - gap, 1.0) - pick(reach - gap, 0.5) - pick(256 - reach - gap, 0.5))
            + ahead * (pick(gap, 1.0) - pick(reach + gap, 0.5) - pick(past, 0.5))
        )
        high, low = split(full)
        quart = (TAU * tree).astype(jnp.bfloat16)
        for slot, table in enumerate((high, high, low, quart, quart)):
            left_ref[grid, rows, slot * 256 + half * 128 : slot * 256 + half * 128 + 128] = table
        near = jnp.minimum(apart, 256 - apart).astype(jnp.float32)
        hat = jnp.where(other == 0, jnp.maximum(0.0, 1.0 - near * slope), 0.0).astype(jnp.bfloat16)
        lanes = slice(half * 128, half * 128 + 128)
        hat_ref[grid, rows, lanes] = hat
        hat_ref[grid, pl.ds(pl.multiple_of(256 + step * 32, 32), 32), lanes] = hat


def class_weights(grid, lv_ref, vel_ref, scale):
    m = lv_ref[grid, 1] - 5
    rows = jnp.left_shift(1, m).astype(jnp.float32)
    weights = stencil(vel_ref[grid, 1] * rows * 0.125)
    return [[jnp.where(m == c, scale * w, 0.0) for w in weights] for c in range(4)]


class Sums:
    def __init__(self):
        self.held = {}

    def add(self, offset, number, value):
        key = (offset, number)
        self.held[key] = value if key not in self.held else self.held[key] + value


def spread(blocks, weights, own, up, down):
    for c in range(4):
        centre, behind, ahead = weights[c]
        count = 1 << c
        per = 8 >> c
        for n in range(per):
            w = [blocks[k * per + n] for k in range(count)]
            moved = []
            for k in range(count):
                value = centre * w[k]
                if k > 0:
                    value += behind * w[k - 1]
                if k < count - 1:
                    value += ahead * w[k + 1]
                moved.append(value)
            above, below = behind * w[-1], ahead * w[0]
            line = moved + [above]
            own.add(0, n, moved[0])
            up.add(0, n, above)
            if count == 1:
                down.add(0, n, below)
            for k in range(1, count):
                s = k & -k
                own.add(k * 8 // count, n, line[k] - 0.5 * (line[k - s] + line[k + s]))
            level = 2
            while level <= count:
                up.add(8 // level, n, -0.5 * above)
                spill = -0.5 * moved[0]
                if level == count:
                    spill += below
                down.add(8 - 8 // level, n, spill)
                level *= 2


def contribute(chunk, lv_ref, vel_ref, coef_ref, w_ref, total_ref, up_ref, down_ref):
    half, quarter = chunk // QUARTERS, chunk % QUARTERS
    own, up, down = Sums(), Sums(), Sums()
    for grid in range(2):
        weights = class_weights(grid, lv_ref, vel_ref, coef_ref[grid].astype(jnp.float32))
        blocks = [
            w_ref[grid, half, pl.ds(pl.multiple_of(quarter * 64 + 8 * n, 8), 8), :] for n in range(8)
        ]
        spread(blocks, weights, own, up, down)
    for offset, (start, count) in BLOCKS.items():
        for n in range(count):
            at = 8 * (start + n)
            total_ref[chunk, at : at + 8, :] = own.held[offset, n]
            if offset in UP:
                up_ref[chunk, at - UP_ROWS[0] : at - UP_ROWS[0] + 8, :] = up.held[offset, n]
            if offset in DOWN:
                down_ref[chunk, at - DOWN_ROWS[0] : at - DOWN_ROWS[0] + 8, :] = down.held[offset, n]


def interpolate(chunk, lv_ref, vel_ref, all_ref, prev_ref, next_ref, g_ref):
    half, quarter = chunk // QUARTERS, chunk % QUARTERS

    def held(offset, n):
        at = 8 * (BLOCKS[offset][0] + n)
        return all_ref[chunk, at : at + 8, :]

    def before(offset, n):
        at = 8 * (BLOCKS[offset][0] + n) - DOWN_ROWS[0]
        return prev_ref[chunk, at : at + 8, :]

    weights = [class_weights(grid, lv_ref, vel_ref, 1.0) for grid in range(2)]
    sums = [Sums(), Sums()]
    for n in range(8):
        node = {0: held(0, n), 8: next_ref[chunk, 8 * n : 8 * n + 8, :]}
        back = {1: before(0, n)}
        last = back[1]
        for c in range(1, 4):
            if n >= 8 >> c:
                break
            s = 8 >> c
            for k in range(1, 1 << c, 2):
                node[k * s] = held(k * s, n) + 0.5 * (node[k * s - s] + node[k * s + s])
            last = before(8 - s, n) + 0.5 * (last + node[0])
            back[1 << c] = last
        for c in range(4):
            per = 8 >> c
            if n >= per:
                break
            count = 1 << c
            line = [back[count]] + [node[k * per] for k in range(count + 1)]
            for k in range(count):
                for grid in range(2):
                    centre, behind, ahead = weights[grid][c]
                    sums[grid].add(
                        0, k * per + n, centre * line[k + 1] + behind * line[k] + ahead * line[k + 2]
                    )
    for grid in range(2):
        for n in range(8):
            at = pl.ds(pl.multiple_of(quarter * 64 + 8 * n, 8), 8)
            g_ref[grid, half, at, :] = sums[grid].held[0, n]


def kernel(
    nz, nd,
    lv_hbm, vel_hbm, rate_hbm, coef_hbm, v_hbm, s_hbm, out_hbm,
    lv_ref, vel_ref, rate_ref, coef_ref, v_ref, s_ref, left_ref, right_ref, hat_ref, w_ref,
    total_ref, up_ref, down_ref, up_in, down_in, minus_in, plus_in,
    all_ref, prev_ref, next_ref, g_ref, out_ref,
    small_sem, load_sem, store_sem, up_sem, down_sem, minus_sem, plus_sem, gminus_sem, gplus_sem, prev_sem, next_sem,
):
    z, d = lax.axis_index("grid"), lax.axis_index("dom")
    north, south = (lax.rem(z + 1, nz), d), (lax.rem(z + nz - 1, nz), d)
    after, ahead_of = (z, lax.rem(d + 1, nd)), (z, lax.rem(d + nd - 1, nd))
    small = [
        pltpu.make_async_copy(source, target, small_sem.at[n])
        for n, (source, target) in enumerate(
            ((lv_hbm, lv_ref), (vel_hbm, vel_ref), (rate_hbm, rate_ref), (coef_hbm, coef_ref))
        )
    ]
    for copy in small:
        copy.start()
    loads = []
    for grid in range(2):
        for n, (source, target) in enumerate(((v_hbm, v_ref), (s_hbm, s_ref))):
            loads.append(pltpu.make_async_copy(source.at[grid], target.at[grid], load_sem.at[grid, n]))
            loads[-1].start()

    barrier = pltpu.get_barrier_semaphore()
    for peer in (north, south, after, ahead_of):
        pl.semaphore_signal(barrier, inc=1, device_id=peer, device_id_type=MESH)

    def remote(source, target, sems, slot, peer):
        return pltpu.make_async_remote_copy(
            src_ref=source, dst_ref=target, send_sem=sems.at[0, slot], recv_sem=sems.at[1, slot],
            device_id=peer, device_id_type=MESH,
        )

    for copy in small:
        copy.wait()
    for grid in range(2):
        @pl.loop(0, 8)
        def _(step):
            build_tables(grid, step, lv_ref, vel_ref, rate_ref, left_ref, hat_ref)

    for grid in range(2):
        loads[2 * grid].wait()
        loads[2 * grid + 1].wait()
        vh, vl = split(v_ref[grid])
        sh, sl = split(s_ref[grid])
        for slot, part in enumerate((vh, vl, vh, sh, sl)):
            right_ref[grid, :, slot * 256 : slot * 256 + 256] = part
        w = dot(left_ref[grid], right_ref[grid], ((1,), (1,)))
        w_ref[grid, 0] = w[:, :128]
        w_ref[grid, 1] = w[:, 128:]

    pl.semaphore_wait(barrier, 4)

    def up_copy(chunk):
        return remote(up_ref.at[chunk], up_in.at[chunk], up_sem, chunk, after)

    def down_copy(chunk):
        return remote(down_ref.at[chunk], down_in.at[chunk], down_sem, chunk, ahead_of)

    far = nz // 2

    @pl.loop(0, nz)
    def _(i):
        off = jnp.where(i % 2 == 0, nz - far + i // 2, far - 1 - (i - 1) // 2)
        chunk = lax.rem(z + off, nz)
        contribute(chunk, lv_ref, vel_ref, coef_ref, w_ref, total_ref, up_ref, down_ref)
        up_copy(chunk).start()
        down_copy(chunk).start()

    def gather_in(chunk, *others):
        up_copy(chunk).wait_recv()
        down_copy(chunk).wait_recv()
        u, w, x = UP_ROWS[1], DOWN_ROWS[0], DOWN_ROWS[0] + DOWN_ROWS[1]

        def at(low, high, value):
            for o in others:
                value = value + o[low:high, :]
            return value

        total_ref[chunk, 0:w, :] = at(0, w, total_ref[chunk, 0:w, :] + up_in[chunk, 0:w, :])
        total_ref[chunk, w:u, :] = at(
            w, u, total_ref[chunk, w:u, :] + up_in[chunk, w:u, :] + down_in[chunk, 0 : u - w, :]
        )
        total_ref[chunk, u:x, :] = at(u, x, total_ref[chunk, u:x, :] + down_in[chunk, u - w : x - w, :])
        if others:
            total_ref[chunk, x:160, :] = at(x, 160, total_ref[chunk, x:160, :])

    def minus_copy(chunk, t):
        return remote(total_ref.at[chunk], minus_in.at[t], minus_sem, t, south)

    def plus_copy(chunk, t):
        return remote(total_ref.at[chunk], plus_in.at[t], plus_sem, t, north)

    for t in range(far):
        chunk = lax.rem(z + nz - far + t, nz)
        if t == 0:
            gather_in(chunk)
        else:
            minus_copy(chunk, t - 1).wait_recv()
            gather_in(chunk, minus_in.at[t - 1])
        minus_copy(chunk, t).start()
        if t < far - 1:
            chunk = lax.rem(z + far - 1 - t, nz)
            if t == 0:
                gather_in(chunk)
            else:
                plus_copy(chunk, t - 1).wait_recv()
                gather_in(chunk, plus_in.at[t - 1])
            plus_copy(chunk, t).start()
    minus_copy(z, far - 1).wait_recv()
    plus_copy(z, far - 2).wait_recv()
    gather_in(z, minus_in.at[far - 1], plus_in.at[far - 2])

    def prev_copy(chunk, source):
        return remote(
            source.at[chunk, DOWN_ROWS[0] : DOWN_ROWS[0] + DOWN_ROWS[1], :], prev_ref.at[chunk], prev_sem, chunk, after
        )

    def next_copy(chunk, source):
        return remote(
            source.at[chunk, FIRST_ROWS[0] : FIRST_ROWS[0] + FIRST_ROWS[1], :], next_ref.at[chunk], next_sem, chunk,
            ahead_of,
        )

    def gminus_copy(chunk, t, source):
        return remote(source.at[chunk], all_ref.at[chunk], gminus_sem, t, south)

    def gplus_copy(chunk, t, source):
        return remote(source.at[chunk], all_ref.at[chunk], gplus_sem, t, north)

    gminus_copy(z, 0, total_ref).start()
    gplus_copy(z, 0, total_ref).start()
    prev_copy(z, total_ref).start()
    next_copy(z, total_ref).start()
    all_ref[z] = total_ref[z]
    for t in range(1, far + 1):
        chunk = lax.rem(z + t, nz)
        gminus_copy(chunk, t - 1, all_ref).wait_recv()
        if t < far:
            gminus_copy(chunk, t, all_ref).start()
        prev_copy(chunk, all_ref).start()
        next_copy(chunk, all_ref).start()
        if t < far:
            chunk = lax.rem(z + nz - t, nz)
            gplus_copy(chunk, t - 1, all_ref).wait_recv()
            if t < far - 1:
                gplus_copy(chunk, t, all_ref).start()
            prev_copy(chunk, all_ref).start()
            next_copy(chunk, all_ref).start()

    @pl.loop(0, nz)
    def _(i):
        off = jnp.where(i % 2 == 0, nz - i // 2, (i + 1) // 2)
        chunk = lax.rem(z + off, nz)
        prev_copy(chunk, all_ref).wait_recv()
        next_copy(chunk, all_ref).wait_recv()
        interpolate(chunk, lv_ref, vel_ref, all_ref, prev_ref, next_ref, g_ref)

    stores = []
    for half in range(2):
        for grid in range(2):
            turned = jnp.transpose(g_ref[grid, half])
            high, low = split(turned)
            lanes = jnp.concatenate([high, low], axis=1)
            out_ref[grid, half * 128 : half * 128 + 128, :] = dot(lanes, hat_ref[grid], ((1,), (0,)))
            rows = slice(half * 128, half * 128 + 128)
            stores.append(
                pltpu.make_async_copy(
                    out_ref.at[grid, rows, :], out_hbm.at[grid, rows, :], store_sem.at[grid, half]
                )
            )
            stores[-1].start()

    @pl.loop(0, nz)
    def _(chunk):
        up_copy(chunk).wait_send()
        down_copy(chunk).wait_send()
        prev_copy(chunk, all_ref).wait_send()
        next_copy(chunk, all_ref).wait_send()

    for t in range(far):
        minus_copy(0, t).wait_send()
        gminus_copy(0, t, all_ref).wait_send()
        if t < far - 1:
            plus_copy(0, t).wait_send()
            gplus_copy(0, t, all_ref).wait_send()
    for store in stores:
        store.wait()


def local(nz, nd, nodal_values, source_term, velocity, react_rate, levels, comb_coefs):
    far = nz // 2
    f32, bf16 = jnp.float32, jnp.bfloat16
    hbm = pl.BlockSpec(memory_space=pl.ANY)
    sem = pltpu.SemaphoreType.DMA
    return pl.pallas_call(
        functools.partial(kernel, nz, nd),
        out_shape=jax.ShapeDtypeStruct((2, 256, 256), f32),
        in_specs=[hbm] * 6,
        out_specs=hbm,
        scratch_shapes=[
            pltpu.SMEM((2, 2), jnp.int32),
            pltpu.SMEM((2, 2), f32),
            pltpu.SMEM((2,), f32),
            pltpu.SMEM((2,), jnp.int32),
            pltpu.VMEM((2, 256, 256), f32),
            pltpu.VMEM((2, 256, 256), f32),
            pltpu.VMEM((2, 256, KDIM), bf16),
            pltpu.VMEM((2, 256, KDIM), bf16),
            pltpu.VMEM((2, 512, 256), bf16),
            pltpu.VMEM((2, 2, 256, 128), f32),
            pltpu.VMEM((nz, 160, 128), f32),
            pltpu.VMEM((nz, 120, 128), f32),
            pltpu.VMEM((nz, 120, 128), f32),
            pltpu.VMEM((nz, 120, 128), f32),
            pltpu.VMEM((nz, 120, 128), f32),
            pltpu.VMEM((far, 160, 128), f32),
            pltpu.VMEM((far - 1, 160, 128), f32),
            pltpu.VMEM((nz, 160, 128), f32),
            pltpu.VMEM((nz, 120, 128), f32),
            pltpu.VMEM((nz, 64, 128), f32),
            pltpu.VMEM((2, 2, 256, 128), f32),
            pltpu.VMEM((2, 256, 256), f32),
            sem((4,)),
            sem((2, 2)),
            sem((2, 2)),
            sem((2, nz)),
            sem((2, nz)),
            sem((2, far)),
            sem((2, far)),
            sem((2, far)),
            sem((2, far)),
            sem((2, nz)),
            sem((2, nz)),
        ],
        compiler_params=pltpu.CompilerParams(collective_id=0, has_side_effects=True, vmem_limit_bytes=67043328),
    )(levels, velocity, react_rate, comb_coefs, nodal_values, source_term)


def solution(mesh):
    in_specs = (
        P("grid", None, "dom"),
        P("grid", None, "dom"),
        P("grid", None),
        P("grid"),
        P("grid", None),
        P("grid"),
    )
    body = functools.partial(local, mesh.shape["grid"], mesh.shape["dom"])
    return jax.shard_map(body, mesh=mesh, in_specs=in_specs, out_specs=P("grid", None, "dom"), check_vma=False)
```

```python
import functools

import jax
import jax.numpy as jnp
from jax import lax
from jax.experimental import pallas as pl
from jax.experimental.pallas import tpu as pltpu
from jax.sharding import PartitionSpec as P

TAU = 0.25
MESH = pl.DeviceIdType.MESH
BLOCKS = {2: (0, 2), 1: (2, 1), 0: (3, 8), 4: (11, 4), 6: (15, 2), 7: (17, 1), 3: (18, 1), 5: (19, 1)}
UP = (2, 1, 0, 4)
DOWN = (0, 4, 6, 7)
UP_ROWS = (0, 120)
DOWN_ROWS = (24, 120)
QUARTERS = 4
FAR = 1 << 20
KDIM = 1280


def dot(left, right, dims):
    return lax.dot_general(left, right, (dims, ((), ())), preferred_element_type=jnp.float32)


def split(value):
    high = value.astype(jnp.bfloat16)
    return high, (value - high.astype(jnp.float32)).astype(jnp.bfloat16)


def stencil(courant):
    square = courant * courant
    return 1.0 - square, 0.5 * (square + courant), 0.5 * (square - courant)


def build_tables(grid, step, lv_ref, vel_ref, rate_ref, left_ref, hat_ref):
    lx, m = lv_ref[grid, 0], lv_ref[grid, 1] - 5
    cols = jnp.left_shift(1, lx)
    gap = jnp.left_shift(1, 8 - lx)
    keep = 1.0 - TAU * rate_ref[grid]
    centre, behind, ahead = stencil(vel_ref[grid, 0] * cols.astype(jnp.float32) * (1.0 / 256.0))
    centre, behind, ahead = keep * centre, keep * behind, keep * ahead

    q = lax.broadcasted_iota(jnp.int32, (32, 128), 0) + step * 32
    quarter = jnp.right_shift(q, 6)
    t = q & 63
    row = jnp.right_shift(t, 6 - m)
    j = t & (jnp.right_shift(64, m) - 1)
    place = 64 * quarter + jnp.where(
        j < 8, 8 * j, jnp.where(j < 16, 8 * j - 60, jnp.where(j < 32, 4 * j - 62, 2 * j - 63))
    )
    reach = jnp.where(j < 8, FAR, jnp.where(j < 16, 4, jnp.where(j < 32, 2, 1)))
    slope = jnp.where(j < 8, 0.125, jnp.where(j < 16, 0.25, jnp.where(j < 32, 0.5, 1.0)))
    row_key = jnp.left_shift(jnp.where(j < jnp.right_shift(cols, 2), row, 1 << 12), 8)
    past = 256 - reach + gap
    past = jnp.where(past == 256, 0, past)
    rows = pl.ds(pl.multiple_of(step * 32, 32), 32)
    for half in range(2):
        p = lax.broadcasted_iota(jnp.int32, (1, 128), 1) + 128 * half
        at = jnp.left_shift(p & (cols - 1), 8 - lx)
        key = jnp.left_shift(jnp.right_shift(p, lx), 8)
        other = key ^ row_key
        apart = (at - place) & 255
        delta = apart | other

        def pick(target, weight):
            return jnp.where(delta == target, weight, 0.0)

        here, right, left = delta == 0, delta == reach, delta == 256 - reach
        tree = jnp.where(here, 1.0, 0.0) - jnp.where(right, 0.5, 0.0) - jnp.where(left, 0.5, 0.0)
        full = (
            centre * tree
            + behind * (pick(256 - gap, 1.0) - pick(reach - gap, 0.5) - pick(256 - reach - gap, 0.5))
            + ahead * (pick(gap, 1.0) - pick(reach + gap, 0.5) - pick(past, 0.5))
        )
        high, low = split(full)
        quart = (TAU * tree).astype(jnp.bfloat16)
        for slot, table in enumerate((high, high, low, quart, quart)):
            left_ref[grid, rows, slot * 256 + half * 128 : slot * 256 + half * 128 + 128] = table
        near = jnp.minimum(apart, 256 - apart).astype(jnp.float32)
        hat = jnp.where(other == 0, jnp.maximum(0.0, 1.0 - near * slope), 0.0).astype(jnp.bfloat16)
        lanes = slice(half * 128, half * 128 + 128)
        hat_ref[grid, rows, lanes] = hat
        hat_ref[grid, pl.ds(pl.multiple_of(256 + step * 32, 32), 32), lanes] = hat


def class_weights(grid, lv_ref, vel_ref):
    m = lv_ref[grid, 1] - 5
    rows = jnp.left_shift(1, m).astype(jnp.float32)
    weights = stencil(vel_ref[grid, 1] * rows * 0.125)
    return [[jnp.where(m == c, w, 0.0) for w in weights] for c in range(4)]


class Sums:
    def __init__(self):
        self.held = {}

    def add(self, offset, number, value):
        key = (offset, number)
        self.held[key] = value if key not in self.held else self.held[key] + value


def spread(blocks, weights, own, up, down):
    for c in range(4):
        centre, behind, ahead = weights[c]
        count = 1 << c
        per = 8 >> c
        for n in range(per):
            w = [blocks[k * per + n] for k in range(count)]
            moved = []
            for k in range(count):
                value = centre * w[k]
                if k > 0:
                    value += behind * w[k - 1]
                if k < count - 1:
                    value += ahead * w[k + 1]
                moved.append(value)
            above, below = behind * w[-1], ahead * w[0]
            line = moved + [above]
            own.add(0, n, moved[0])
            up.add(0, n, above)
            if count == 1:
                down.add(0, n, below)
            for k in range(1, count):
                s = k & -k
                own.add(k * 8 // count, n, line[k] - 0.5 * (line[k - s] + line[k + s]))
            level = 2
            while level <= count:
                up.add(8 // level, n, -0.5 * above)
                spill = -0.5 * moved[0]
                if level == count:
                    spill += below
                down.add(8 - 8 // level, n, spill)
                level *= 2


def contribute(first, weights_row, blocks_ref, at, own_ref, up_ref, down_ref):
    own, up, down = Sums(), Sums(), Sums()
    for grid in range(2):
        blocks = [blocks_ref[at, grid, 8 * n : 8 * n + 8, :] for n in range(8)]
        spread(blocks, weights_of(weights_row, grid), own, up, down)
    for offset, (start, count) in BLOCKS.items():
        for n in range(count):
            low = 8 * (start + n)
            targets = [(own_ref, low, own)]
            if offset in UP:
                targets.append((up_ref, low - UP_ROWS[0], up))
            if offset in DOWN:
                targets.append((down_ref, low - DOWN_ROWS[0], down))
            for ref, row, sums in targets:
                value = sums.held[offset, n]
                ref[row : row + 8, :] = value if first else ref[row : row + 8, :] + value


def weights_of(row, grid):
    return [
        [jnp.broadcast_to(row[:, 12 * grid + 3 * c + n : 12 * grid + 3 * c + n + 1], (8, 128)) for n in range(3)]
        for c in range(4)
    ]


def make_nodes(own_ref, up_ref, down_ref, halo, node_ref, next_ref, back_ref):
    prev_in, up_in, up_far, first_in, down_in, down_far = halo

    def block(ref, n):
        return ref[8 * n : 8 * n + 8, :]

    def held(offset, n):
        at = BLOCKS[offset][0] + n
        value = block(own_ref, at)
        if offset in UP:
            value += block(up_in, at)
        if offset in DOWN:
            value += block(down_in, at - 3)
        return value

    def before(offset, n):
        at = BLOCKS[offset][0] + n - 3
        value = block(prev_in, at) + block(down_ref, at)
        return value + block(up_far, at) if offset in (0, 4) else value

    for n in range(8):
        node = {0: held(0, n), 8: block(first_in, n) + block(up_ref, 3 + n) + block(down_far, n)}
        last = before(0, n)
        back_ref[0, n] = last
        next_ref[n] = node[8]
        node_ref[0, n] = node[0]
        for c in range(1, 4):
            if n >= 8 >> c:
                break
            s = 8 >> c
            for k in range(1, 1 << c, 2):
                node[k * s] = held(k * s, n) + 0.5 * (node[k * s - s] + node[k * s + s])
                node_ref[k * s, n] = node[k * s]
            last = before(8 - s, n) + 0.5 * (last + node[0])
            back_ref[c, n] = last


def interpolate(weights_row, node_ref, next_ref, back_ref, g_ref, at):
    weights = [weights_of(weights_row, grid) for grid in range(2)]
    sums = [Sums(), Sums()]
    for c in range(4):
        per = 8 >> c
        count = 1 << c
        for n in range(per):
            line = [back_ref[c, n]] + [node_ref[k * per, n] for k in range(count)] + [next_ref[n]]
            for k in range(count):
                for grid in range(2):
                    centre, behind, ahead = weights[grid][c]
                    sums[grid].add(
                        0, k * per + n, centre * line[k + 1] + behind * line[k] + ahead * line[k + 2]
                    )
    for grid in range(2):
        for n in range(8):
            g_ref[at, grid, 8 * n : 8 * n + 8, :] = sums[grid].held[0, n]


def kernel(
    nz, nd,
    lv_hbm, vel_hbm, rate_hbm, coef_hbm, v_hbm, s_hbm, out_hbm,
    lv_ref, vel_ref, rate_ref, coef_ref, v_ref, s_ref, left_ref, right_ref, hat_ref,
    w_ref, w_in, row_ref, row_in, own_ref, up_ref, down_ref,
    prev_in, up_in, up_far, first_in, down_in, down_far,
    node_ref, next_ref, back_ref, g_ref, g_in, out_ref,
    small_sem, load_sem, store_sem, w_sem, row_sem, halo_sem, g_sem,
):
    z, d = lax.axis_index("grid"), lax.axis_index("dom")
    small = [
        pltpu.make_async_copy(source, target, small_sem.at[n])
        for n, (source, target) in enumerate(
            ((lv_hbm, lv_ref), (vel_hbm, vel_ref), (rate_hbm, rate_ref), (coef_hbm, coef_ref))
        )
    ]
    for copy in small:
        copy.start()
    loads = []
    for grid in range(2):
        for n, (source, target) in enumerate(((v_hbm, v_ref), (s_hbm, s_ref))):
            loads.append(pltpu.make_async_copy(source.at[grid], target.at[grid], load_sem.at[grid, n]))
            loads[-1].start()

    barrier = pltpu.get_barrier_semaphore()
    peers = [(lax.rem(z + n, nz), d) for n in range(1, nz)]
    peers += [(z, lax.rem(d + n, nd)) for n in (1, 2, nd - 1, nd - 2)]
    for peer in peers:
        pl.semaphore_signal(barrier, inc=1, device_id=peer, device_id_type=MESH)

    def remote(source, target, send, recv, peer):
        return pltpu.make_async_remote_copy(
            src_ref=source, dst_ref=target, send_sem=send, recv_sem=recv, device_id=peer, device_id_type=MESH
        )

    def far_first(i):
        return lax.rem(z + jnp.where(i % 2 == 0, nz // 2 + i // 2, nz // 2 - 1 - (i - 1) // 2), nz)

    for copy in small:
        copy.wait()
    lane = lax.broadcasted_iota(jnp.int32, (1, 128), 1)
    row = jnp.zeros((1, 128), jnp.float32)
    for grid in range(2):
        for c, weights in enumerate(class_weights(grid, lv_ref, vel_ref)):
            for n, weight in enumerate(weights):
                row = jnp.where(lane == 12 * grid + 3 * c + n, weight, row)
    row_ref[...] = row
    for grid in range(2):
        @pl.loop(0, 8)
        def _(step):
            build_tables(grid, step, lv_ref, vel_ref, rate_ref, left_ref, hat_ref)

    for grid in range(2):
        loads[2 * grid].wait()
        loads[2 * grid + 1].wait()
        vh, vl = split(v_ref[grid])
        sh, sl = split(s_ref[grid])
        for slot, part in enumerate((vh, vl, vh, sh, sl)):
            right_ref[grid, :, slot * 256 : slot * 256 + 256] = part
        w = dot(left_ref[grid], right_ref[grid], ((1,), (1,))) * coef_ref[grid].astype(jnp.float32)
        for half in range(2):
            for quarter in range(QUARTERS):
                w_ref[half * QUARTERS + quarter, grid] = w[
                    quarter * 64 : quarter * 64 + 64, half * 128 : half * 128 + 128
                ]

    pl.semaphore_wait(barrier, len(peers))

    def w_copy(slot, target, peer):
        return remote(w_ref.at[peer], w_in.at[slot], w_sem.at[0, peer], w_sem.at[1, slot], (target, d))

    def row_copy(slot, target, peer):
        return remote(row_ref, row_in.at[slot], row_sem.at[0, peer], row_sem.at[1, slot], (target, d))

    @pl.loop(0, nz - 1)
    def _(i):
        peer = far_first(i)
        row_copy(z, peer, peer).start()
        w_copy(z, peer, peer).start()

    contribute(True, row_ref[...], w_ref, z, own_ref, up_ref, down_ref)

    @pl.loop(0, nz - 1)
    def _(i):
        peer = far_first(nz - 2 - i)
        row_copy(peer, peer, peer).wait_recv()
        w_copy(peer, peer, peer).wait_recv()
        contribute(False, row_in[peer], w_in, peer, own_ref, up_ref, down_ref)

    def halo_copy(n, source, target, step):
        return remote(source, target, halo_sem.at[0, n], halo_sem.at[1, n], (z, lax.rem(d + nd + step, nd)))

    halos = [
        halo_copy(0, up_ref.at[24:120, :], up_far, 2),
        halo_copy(1, down_ref.at[0:64, :], down_far, -2),
        halo_copy(2, own_ref.at[24:144, :], prev_in, 1),
        halo_copy(3, own_ref.at[24:88, :], first_in, -1),
        halo_copy(4, up_ref, up_in, 1),
        halo_copy(5, down_ref, down_in, -1),
    ]
    for copy in halos:
        copy.start()
    for copy in halos:
        copy.wait_recv()
    make_nodes(
        own_ref, up_ref, down_ref, (prev_in, up_in, up_far, first_in, down_in, down_far),
        node_ref, next_ref, back_ref,
    )

    def g_copy(slot, target, peer):
        return remote(g_ref.at[peer], g_in.at[slot], g_sem.at[0, peer], g_sem.at[1, slot], (target, d))

    @pl.loop(0, nz - 1)
    def _(i):
        peer = far_first(i)
        interpolate(row_in[peer], node_ref, next_ref, back_ref, g_ref, peer)
        g_copy(z, peer, peer).start()

    interpolate(row_ref[...], node_ref, next_ref, back_ref, g_in, z)

    @pl.loop(0, nz - 1)
    def _(i):
        peer = far_first(nz - 2 - i)
        g_copy(peer, peer, peer).wait_recv()

    stores = []
    for half in range(2):
        for grid in range(2):
            turned = jnp.transpose(
                jnp.concatenate([g_in[half * QUARTERS + n, grid] for n in range(QUARTERS)], axis=0)
            )
            high, low = split(turned)
            lanes = jnp.concatenate([high, low], axis=1)
            rows = slice(half * 128, half * 128 + 128)
            out_ref[grid, rows, :] = dot(lanes, hat_ref[grid], ((1,), (0,)))
            stores.append(
                pltpu.make_async_copy(
                    out_ref.at[grid, rows, :], out_hbm.at[grid, rows, :], store_sem.at[grid, half]
                )
            )
            stores[-1].start()

    for copy in halos:
        copy.wait_send()

    @pl.loop(0, nz - 1)
    def _(i):
        peer = far_first(i)
        row_copy(z, peer, peer).wait_send()
        w_copy(z, peer, peer).wait_send()
        g_copy(z, peer, peer).wait_send()

    for store in stores:
        store.wait()


def local(nz, nd, nodal_values, source_term, velocity, react_rate, levels, comb_coefs):
    f32, bf16 = jnp.float32, jnp.bfloat16
    hbm = pl.BlockSpec(memory_space=pl.ANY)
    sem = pltpu.SemaphoreType.DMA
    return pl.pallas_call(
        functools.partial(kernel, nz, nd),
        out_shape=jax.ShapeDtypeStruct((2, 256, 256), f32),
        in_specs=[hbm] * 6,
        out_specs=hbm,
        scratch_shapes=[
            pltpu.SMEM((2, 2), jnp.int32),
            pltpu.SMEM((2, 2), f32),
            pltpu.SMEM((2,), f32),
            pltpu.SMEM((2,), jnp.int32),
            pltpu.VMEM((2, 256, 256), f32),
            pltpu.VMEM((2, 256, 256), f32),
            pltpu.VMEM((2, 256, KDIM), bf16),
            pltpu.VMEM((2, 256, KDIM), bf16),
            pltpu.VMEM((2, 512, 256), bf16),
            pltpu.VMEM((nz, 2, 64, 128), f32),
            pltpu.VMEM((nz, 2, 64, 128), f32),
            pltpu.VMEM((1, 128), f32),
            pltpu.VMEM((nz, 1, 128), f32),
            pltpu.VMEM((160, 128), f32),
            pltpu.VMEM((120, 128), f32),
            pltpu.VMEM((120, 128), f32),
            pltpu.VMEM((120, 128), f32),
            pltpu.VMEM((120, 128), f32),
            pltpu.VMEM((96, 128), f32),
            pltpu.VMEM((64, 128), f32),
            pltpu.VMEM((120, 128), f32),
            pltpu.VMEM((64, 128), f32),
            pltpu.VMEM((8, 8, 8, 128), f32),
            pltpu.VMEM((8, 8, 128), f32),
            pltpu.VMEM((4, 8, 8, 128), f32),
            pltpu.VMEM((nz, 2, 64, 128), f32),
            pltpu.VMEM((nz, 2, 64, 128), f32),
            pltpu.VMEM((2, 256, 256), f32),
            sem((4,)),
            sem((2, 2)),
            sem((2, 2)),
            sem((2, nz)),
            sem((2, nz)),
            sem((2, 6)),
            sem((2, nz)),
        ],
        compiler_params=pltpu.CompilerParams(collective_id=0, has_side_effects=True, vmem_limit_bytes=67043328),
    )(levels, velocity, react_rate, comb_coefs, nodal_values, source_term)


def solution(mesh):
    in_specs = (
        P("grid", None, "dom"),
        P("grid", None, "dom"),
        P("grid", None),
        P("grid"),
        P("grid", None),
        P("grid"),
    )
    body = functools.partial(local, mesh.shape["grid"], mesh.shape["dom"])
    return jax.shard_map(body, mesh=mesh, in_specs=in_specs, out_specs=P("grid", None, "dom"), check_vma=False)
```

```python
import functools

import jax
import jax.numpy as jnp
from jax import lax
from jax.experimental import pallas as pl
from jax.experimental.pallas import tpu as pltpu
from jax.sharding import PartitionSpec as P

TAU = 0.25
MESH = pl.DeviceIdType.MESH
BLOCKS = {2: (0, 2), 1: (2, 1), 0: (3, 8), 4: (11, 4), 6: (15, 2), 7: (17, 1), 3: (18, 1), 5: (19, 1)}
UP = (2, 1, 0, 4)
DOWN = (0, 4, 6, 7)
UP_ROWS = (0, 120)
DOWN_ROWS = (24, 120)
QUARTERS = 4
FAR = 1 << 20
KDIM = 1280


def dot(left, right, dims):
    return lax.dot_general(left, right, (dims, ((), ())), preferred_element_type=jnp.float32)


def split(value):
    high = value.astype(jnp.bfloat16)
    return high, (value - high.astype(jnp.float32)).astype(jnp.bfloat16)


def stencil(courant):
    square = courant * courant
    return 1.0 - square, 0.5 * (square + courant), 0.5 * (square - courant)


def build_tables(grid, step, lv_ref, vel_ref, rate_ref, left_ref, hat_ref):
    lx, m = lv_ref[grid, 0], lv_ref[grid, 1] - 5
    cols = jnp.left_shift(1, lx)
    gap = jnp.left_shift(1, 8 - lx)
    keep = 1.0 - TAU * rate_ref[grid]
    centre, behind, ahead = stencil(vel_ref[grid, 0] * cols.astype(jnp.float32) * (1.0 / 256.0))
    centre, behind, ahead = keep * centre, keep * behind, keep * ahead

    q = lax.broadcasted_iota(jnp.int32, (32, 128), 0) + step * 32
    quarter = jnp.right_shift(q, 6)
    t = q & 63
    row = jnp.right_shift(t, 6 - m)
    j = t & (jnp.right_shift(64, m) - 1)
    place = 64 * quarter + jnp.where(
        j < 8, 8 * j, jnp.where(j < 16, 8 * j - 60, jnp.where(j < 32, 4 * j - 62, 2 * j - 63))
    )
    reach = jnp.where(j < 8, FAR, jnp.where(j < 16, 4, jnp.where(j < 32, 2, 1)))
    slope = jnp.where(j < 8, 0.125, jnp.where(j < 16, 0.25, jnp.where(j < 32, 0.5, 1.0)))
    row_key = jnp.left_shift(jnp.where(j < jnp.right_shift(cols, 2), row, 1 << 12), 8)
    past = 256 - reach + gap
    past = jnp.where(past == 256, 0, past)
    rows = pl.ds(pl.multiple_of(step * 32, 32), 32)
    for half in range(2):
        p = lax.broadcasted_iota(jnp.int32, (1, 128), 1) + 128 * half
        at = jnp.left_shift(p & (cols - 1), 8 - lx)
        key = jnp.left_shift(jnp.right_shift(p, lx), 8)
        other = key ^ row_key
        apart = (at - place) & 255
        delta = apart | other

        def pick(target, weight):
            return jnp.where(delta == target, weight, 0.0)

        here, right, left = delta == 0, delta == reach, delta == 256 - reach
        tree = jnp.where(here, 1.0, 0.0) - jnp.where(right, 0.5, 0.0) - jnp.where(left, 0.5, 0.0)
        full = (
            centre * tree
            + behind * (pick(256 - gap, 1.0) - pick(reach - gap, 0.5) - pick(256 - reach - gap, 0.5))
            + ahead * (pick(gap, 1.0) - pick(reach + gap, 0.5) - pick(past, 0.5))
        )
        high, low = split(full)
        quart = (TAU * tree).astype(jnp.bfloat16)
        for slot, table in enumerate((high, high, low, quart, quart)):
            left_ref[grid, rows, slot * 256 + half * 128 : slot * 256 + half * 128 + 128] = table
        near = jnp.minimum(apart, 256 - apart).astype(jnp.float32)
        hat = jnp.where(other == 0, jnp.maximum(0.0, 1.0 - near * slope), 0.0).astype(jnp.bfloat16)
        lanes = slice(half * 128, half * 128 + 128)
        hat_ref[grid, rows, lanes] = hat
        hat_ref[grid, pl.ds(pl.multiple_of(256 + step * 32, 32), 32), lanes] = hat


def class_weights(grid, lv_ref, vel_ref):
    m = lv_ref[grid, 1] - 5
    rows = jnp.left_shift(1, m).astype(jnp.float32)
    weights = stencil(vel_ref[grid, 1] * rows * 0.125)
    return [[jnp.where(m == c, w, 0.0) for w in weights] for c in range(4)]


class Sums:
    def __init__(self):
        self.held = {}

    def add(self, offset, number, value):
        key = (offset, number)
        self.held[key] = value if key not in self.held else self.held[key] + value


def spread(blocks, weights, own, up, down):
    for c in range(4):
        centre, behind, ahead = weights[c]
        count = 1 << c
        per = 8 >> c
        for n in range(per):
            w = [blocks[k * per + n] for k in range(count)]
            moved = []
            for k in range(count):
                value = centre * w[k]
                if k > 0:
                    value += behind * w[k - 1]
                if k < count - 1:
                    value += ahead * w[k + 1]
                moved.append(value)
            above, below = behind * w[-1], ahead * w[0]
            line = moved + [above]
            own.add(0, n, moved[0])
            up.add(0, n, above)
            if count == 1:
                down.add(0, n, below)
            for k in range(1, count):
                s = k & -k
                own.add(k * 8 // count, n, line[k] - 0.5 * (line[k - s] + line[k + s]))
            level = 2
            while level <= count:
                up.add(8 // level, n, -0.5 * above)
                spill = -0.5 * moved[0]
                if level == count:
                    spill += below
                down.add(8 - 8 // level, n, spill)
                level *= 2


def contribute(first, weights_row, blocks_ref, at, own_ref, up_ref, down_ref):
    own, up, down = Sums(), Sums(), Sums()
    for grid in range(2):
        blocks = [blocks_ref[at, grid, 8 * n : 8 * n + 8, :] for n in range(8)]
        spread(blocks, weights_of(weights_row, grid), own, up, down)
    for offset, (start, count) in BLOCKS.items():
        for n in range(count):
            low = 8 * (start + n)
            targets = [(own_ref, low, own)]
            if offset in UP:
                targets.append((up_ref, low - UP_ROWS[0], up))
            if offset in DOWN:
                targets.append((down_ref, low - DOWN_ROWS[0], down))
            for ref, row, sums in targets:
                value = sums.held[offset, n]
                ref[row : row + 8, :] = value if first else ref[row : row + 8, :] + value


def weights_of(row, grid):
    return [
        [jnp.broadcast_to(row[:, 12 * grid + 3 * c + n : 12 * grid + 3 * c + n + 1], (8, 128)) for n in range(3)]
        for c in range(4)
    ]


def make_nodes(own_ref, up_ref, down_ref, halo, node_ref, next_ref, back_ref):
    prev_in, up_in, up_far, first_in, down_in, down_far = halo

    def block(ref, n):
        return ref[8 * n : 8 * n + 8, :]

    def held(offset, n):
        at = BLOCKS[offset][0] + n
        value = block(own_ref, at)
        if offset in UP:
            value += block(up_in, at)
        if offset in DOWN:
            value += block(down_in, at - 3)
        return value

    def before(offset, n):
        at = BLOCKS[offset][0] + n - 3
        value = block(prev_in, at) + block(down_ref, at)
        return value + block(up_far, at) if offset in (0, 4) else value

    for n in range(8):
        node = {0: held(0, n), 8: block(first_in, n) + block(up_ref, 3 + n) + block(down_far, n)}
        last = before(0, n)
        back_ref[0, n] = last
        next_ref[n] = node[8]
        node_ref[0, n] = node[0]
        for c in range(1, 4):
            if n >= 8 >> c:
                break
            s = 8 >> c
            for k in range(1, 1 << c, 2):
                node[k * s] = held(k * s, n) + 0.5 * (node[k * s - s] + node[k * s + s])
                node_ref[k * s, n] = node[k * s]
            last = before(8 - s, n) + 0.5 * (last + node[0])
            back_ref[c, n] = last


def interpolate(weights_row, node_ref, next_ref, back_ref, g_ref, at):
    weights = [weights_of(weights_row, grid) for grid in range(2)]
    sums = [Sums(), Sums()]
    for c in range(4):
        per = 8 >> c
        count = 1 << c
        for n in range(per):
            line = [back_ref[c, n]] + [node_ref[k * per, n] for k in range(count)] + [next_ref[n]]
            for k in range(count):
                for grid in range(2):
                    centre, behind, ahead = weights[grid][c]
                    sums[grid].add(
                        0, k * per + n, centre * line[k + 1] + behind * line[k] + ahead * line[k + 2]
                    )
    for grid in range(2):
        for n in range(8):
            g_ref[at, grid, 8 * n : 8 * n + 8, :] = sums[grid].held[0, n]


def kernel(
    nz, nd,
    lv_hbm, vel_hbm, rate_hbm, coef_hbm, v_hbm, s_hbm, out_hbm,
    lv_ref, vel_ref, rate_ref, coef_ref, v_ref, s_ref, left_ref, right_ref, hat_ref,
    w_ref, w_in, row_ref, row_in, own_ref, up_ref, down_ref,
    prev_in, up_in, up_far, first_in, down_in, down_far,
    node_ref, next_ref, back_ref, g_ref, g_in, out_ref,
    small_sem, load_sem, store_sem, w_sem, row_sem, halo_sem, g_sem,
):
    z, d = lax.axis_index("grid"), lax.axis_index("dom")
    small = [
        pltpu.make_async_copy(source, target, small_sem.at[n])
        for n, (source, target) in enumerate(
            ((lv_hbm, lv_ref), (vel_hbm, vel_ref), (rate_hbm, rate_ref), (coef_hbm, coef_ref))
        )
    ]
    for copy in small:
        copy.start()
    loads = []
    for grid in range(2):
        for n, (source, target) in enumerate(((v_hbm, v_ref), (s_hbm, s_ref))):
            loads.append(pltpu.make_async_copy(source.at[grid], target.at[grid], load_sem.at[grid, n]))
            loads[-1].start()

    barrier = pltpu.get_barrier_semaphore()
    peers = [(lax.rem(z + n, nz), d) for n in range(1, nz)]
    peers += [(z, lax.rem(d + n, nd)) for n in (1, 2, nd - 1, nd - 2)]
    for peer in peers:
        pl.semaphore_signal(barrier, inc=1, device_id=peer, device_id_type=MESH)

    def remote(source, target, send, recv, peer):
        return pltpu.make_async_remote_copy(
            src_ref=source, dst_ref=target, send_sem=send, recv_sem=recv, device_id=peer, device_id_type=MESH
        )

    def near_first(i):
        return lax.rem(z + jnp.where(i % 2 == 0, 1 + i // 2, nz - (i + 1) // 2), nz)

    for copy in small:
        copy.wait()
    lane = lax.broadcasted_iota(jnp.int32, (1, 128), 1)
    row = jnp.zeros((1, 128), jnp.float32)
    for grid in range(2):
        for c, weights in enumerate(class_weights(grid, lv_ref, vel_ref)):
            for n, weight in enumerate(weights):
                row = jnp.where(lane == 12 * grid + 3 * c + n, weight, row)
    row_ref[...] = row
    for grid in range(2):
        @pl.loop(0, 8)
        def _(step):
            build_tables(grid, step, lv_ref, vel_ref, rate_ref, left_ref, hat_ref)

    for grid in range(2):
        loads[2 * grid].wait()
        loads[2 * grid + 1].wait()
        vh, vl = split(v_ref[grid])
        sh, sl = split(s_ref[grid])
        for slot, part in enumerate((vh, vl, vh, sh, sl)):
            right_ref[grid, :, slot * 256 : slot * 256 + 256] = part
        w = dot(left_ref[grid], right_ref[grid], ((1,), (1,))) * coef_ref[grid].astype(jnp.float32)
        for half in range(2):
            for quarter in range(QUARTERS):
                w_ref[half * QUARTERS + quarter, grid] = w[
                    quarter * 64 : quarter * 64 + 64, half * 128 : half * 128 + 128
                ]

    pl.semaphore_wait(barrier, len(peers))

    def w_copy(slot, target, peer):
        return remote(w_ref.at[peer], w_in.at[slot], w_sem.at[0, peer], w_sem.at[1, slot], (target, d))

    def row_copy(slot, target, peer):
        return remote(row_ref, row_in.at[slot], row_sem.at[0, peer], row_sem.at[1, slot], (target, d))

    @pl.loop(0, nz - 1)
    def _(i):
        peer = near_first(i)
        row_copy(z, peer, peer).start()
        w_copy(z, peer, peer).start()

    contribute(True, row_ref[...], w_ref, z, own_ref, up_ref, down_ref)

    @pl.loop(0, nz - 1)
    def _(i):
        peer = near_first(i)
        row_copy(peer, peer, peer).wait_recv()
        w_copy(peer, peer, peer).wait_recv()
        contribute(False, row_in[peer], w_in, peer, own_ref, up_ref, down_ref)

    def halo_copy(n, source, target, step):
        return remote(source, target, halo_sem.at[0, n], halo_sem.at[1, n], (z, lax.rem(d + nd + step, nd)))

    halos = [
        halo_copy(0, up_ref.at[24:120, :], up_far, 2),
        halo_copy(1, down_ref.at[0:64, :], down_far, -2),
        halo_copy(2, own_ref.at[24:144, :], prev_in, 1),
        halo_copy(3, own_ref.at[24:88, :], first_in, -1),
        halo_copy(4, up_ref, up_in, 1),
        halo_copy(5, down_ref, down_in, -1),
    ]
    for copy in halos:
        copy.start()
    for copy in halos:
        copy.wait_recv()
    make_nodes(
        own_ref, up_ref, down_ref, (prev_in, up_in, up_far, first_in, down_in, down_far),
        node_ref, next_ref, back_ref,
    )

    def g_copy(slot, target, peer):
        return remote(g_ref.at[peer], g_in.at[slot], g_sem.at[0, peer], g_sem.at[1, slot], (target, d))

    @pl.loop(0, nz)
    def _(peer):
        @pl.when(peer != z)
        def _():
            interpolate(row_in[peer], node_ref, next_ref, back_ref, g_ref, peer)
            g_copy(z, peer, peer).start()

    interpolate(row_ref[...], node_ref, next_ref, back_ref, g_in, z)

    stores = []
    for half in range(2):
        @pl.loop(half * QUARTERS, half * QUARTERS + QUARTERS)
        def _(peer):
            @pl.when(peer != z)
            def _():
                g_copy(peer, peer, peer).wait_recv()

        for grid in range(2):
            turned = jnp.transpose(
                jnp.concatenate([g_in[half * QUARTERS + n, grid] for n in range(QUARTERS)], axis=0)
            )
            high, low = split(turned)
            lanes = jnp.concatenate([high, low], axis=1)
            rows = slice(half * 128, half * 128 + 128)
            out_ref[grid, rows, :] = dot(lanes, hat_ref[grid], ((1,), (0,)))
            stores.append(
                pltpu.make_async_copy(
                    out_ref.at[grid, rows, :], out_hbm.at[grid, rows, :], store_sem.at[grid, half]
                )
            )
            stores[-1].start()

    for copy in halos:
        copy.wait_send()

    @pl.loop(0, nz - 1)
    def _(i):
        peer = near_first(i)
        row_copy(z, peer, peer).wait_send()
        w_copy(z, peer, peer).wait_send()
        g_copy(z, peer, peer).wait_send()

    for store in stores:
        store.wait()


def local(nz, nd, nodal_values, source_term, velocity, react_rate, levels, comb_coefs):
    f32, bf16 = jnp.float32, jnp.bfloat16
    hbm = pl.BlockSpec(memory_space=pl.ANY)
    sem = pltpu.SemaphoreType.DMA
    return pl.pallas_call(
        functools.partial(kernel, nz, nd),
        out_shape=jax.ShapeDtypeStruct((2, 256, 256), f32),
        in_specs=[hbm] * 6,
        out_specs=hbm,
        scratch_shapes=[
            pltpu.SMEM((2, 2), jnp.int32),
            pltpu.SMEM((2, 2), f32),
            pltpu.SMEM((2,), f32),
            pltpu.SMEM((2,), jnp.int32),
            pltpu.VMEM((2, 256, 256), f32),
            pltpu.VMEM((2, 256, 256), f32),
            pltpu.VMEM((2, 256, KDIM), bf16),
            pltpu.VMEM((2, 256, KDIM), bf16),
            pltpu.VMEM((2, 512, 256), bf16),
            pltpu.VMEM((nz, 2, 64, 128), f32),
            pltpu.VMEM((nz, 2, 64, 128), f32),
            pltpu.VMEM((1, 128), f32),
            pltpu.VMEM((nz, 1, 128), f32),
            pltpu.VMEM((160, 128), f32),
            pltpu.VMEM((120, 128), f32),
            pltpu.VMEM((120, 128), f32),
            pltpu.VMEM((120, 128), f32),
            pltpu.VMEM((120, 128), f32),
            pltpu.VMEM((96, 128), f32),
            pltpu.VMEM((64, 128), f32),
            pltpu.VMEM((120, 128), f32),
            pltpu.VMEM((64, 128), f32),
            pltpu.VMEM((8, 8, 8, 128), f32),
            pltpu.VMEM((8, 8, 128), f32),
            pltpu.VMEM((4, 8, 8, 128), f32),
            pltpu.VMEM((nz, 2, 64, 128), f32),
            pltpu.VMEM((nz, 2, 64, 128), f32),
            pltpu.VMEM((2, 256, 256), f32),
            sem((4,)),
            sem((2, 2)),
            sem((2, 2)),
            sem((2, nz)),
            sem((2, nz)),
            sem((2, 6)),
            sem((2, nz)),
        ],
        compiler_params=pltpu.CompilerParams(collective_id=0, has_side_effects=True, vmem_limit_bytes=67043328),
    )(levels, velocity, react_rate, comb_coefs, nodal_values, source_term)


def solution(mesh):
    in_specs = (
        P("grid", None, "dom"),
        P("grid", None, "dom"),
        P("grid", None),
        P("grid"),
        P("grid", None),
        P("grid"),
    )
    body = functools.partial(local, mesh.shape["grid"], mesh.shape["dom"])
    return jax.shard_map(body, mesh=mesh, in_specs=in_specs, out_specs=P("grid", None, "dom"), check_vma=False)
```

```python
import functools

import jax
import jax.numpy as jnp
from jax import lax
from jax.experimental import pallas as pl
from jax.experimental.pallas import tpu as pltpu
from jax.sharding import PartitionSpec as P

TAU = 0.25
MESH = pl.DeviceIdType.MESH
BLOCKS = {2: (0, 2), 1: (2, 1), 0: (3, 8), 4: (11, 4), 6: (15, 2), 7: (17, 1), 3: (18, 1), 5: (19, 1)}
UP = (2, 1, 0, 4)
DOWN = (0, 4, 6, 7)
UP_ROWS = (0, 120)
DOWN_ROWS = (24, 120)
QUARTERS = 4
FAR = 1 << 20
KDIM = 1280


def dot(left, right, dims):
    return lax.dot_general(left, right, (dims, ((), ())), preferred_element_type=jnp.float32)


def split(value):
    high = value.astype(jnp.bfloat16)
    return high, (value - high.astype(jnp.float32)).astype(jnp.bfloat16)


def stencil(courant):
    square = courant * courant
    return 1.0 - square, 0.5 * (square + courant), 0.5 * (square - courant)


def build_tables(grid, step, lv_ref, vel_ref, rate_ref, left_ref, hat_ref):
    lx, m = lv_ref[grid, 0], lv_ref[grid, 1] - 5
    cols = jnp.left_shift(1, lx)
    gap = jnp.left_shift(1, 8 - lx)
    keep = 1.0 - TAU * rate_ref[grid]
    centre, behind, ahead = stencil(vel_ref[grid, 0] * cols.astype(jnp.float32) * (1.0 / 256.0))
    centre, behind, ahead = keep * centre, keep * behind, keep * ahead

    q = lax.broadcasted_iota(jnp.int32, (32, 128), 0) + step * 32
    quarter = jnp.right_shift(q, 6)
    t = q & 63
    row = jnp.right_shift(t, 6 - m)
    j = t & (jnp.right_shift(64, m) - 1)
    place = 64 * quarter + jnp.where(
        j < 8, 8 * j, jnp.where(j < 16, 8 * j - 60, jnp.where(j < 32, 4 * j - 62, 2 * j - 63))
    )
    reach = jnp.where(j < 8, FAR, jnp.where(j < 16, 4, jnp.where(j < 32, 2, 1)))
    slope = jnp.where(j < 8, 0.125, jnp.where(j < 16, 0.25, jnp.where(j < 32, 0.5, 1.0)))
    row_key = jnp.left_shift(jnp.where(j < jnp.right_shift(cols, 2), row, 1 << 12), 8)
    past = 256 - reach + gap
    past = jnp.where(past == 256, 0, past)
    rows = pl.ds(pl.multiple_of(step * 32, 32), 32)
    for half in range(2):
        p = lax.broadcasted_iota(jnp.int32, (1, 128), 1) + 128 * half
        at = jnp.left_shift(p & (cols - 1), 8 - lx)
        key = jnp.left_shift(jnp.right_shift(p, lx), 8)
        other = key ^ row_key
        apart = (at - place) & 255
        delta = apart | other

        def pick(target, weight):
            return jnp.where(delta == target, weight, 0.0)

        here, right, left = delta == 0, delta == reach, delta == 256 - reach
        tree = jnp.where(here, 1.0, 0.0) - jnp.where(right, 0.5, 0.0) - jnp.where(left, 0.5, 0.0)
        full = (
            centre * tree
            + behind * (pick(256 - gap, 1.0) - pick(reach - gap, 0.5) - pick(256 - reach - gap, 0.5))
            + ahead * (pick(gap, 1.0) - pick(reach + gap, 0.5) - pick(past, 0.5))
        )
        high, low = split(full)
        quart = (TAU * tree).astype(jnp.bfloat16)
        for slot, table in enumerate((high, high, low, quart, quart)):
            left_ref[grid, rows, slot * 256 + half * 128 : slot * 256 + half * 128 + 128] = table
        near = jnp.minimum(apart, 256 - apart).astype(jnp.float32)
        hat = jnp.where(other == 0, jnp.maximum(0.0, 1.0 - near * slope), 0.0).astype(jnp.bfloat16)
        lanes = slice(half * 128, half * 128 + 128)
        hat_ref[grid, rows, lanes] = hat
        hat_ref[grid, pl.ds(pl.multiple_of(256 + step * 32, 32), 32), lanes] = hat


def class_weights(grid, lv_ref, vel_ref):
    m = lv_ref[grid, 1] - 5
    rows = jnp.left_shift(1, m).astype(jnp.float32)
    weights = stencil(vel_ref[grid, 1] * rows * 0.125)
    return [[jnp.where(m == c, w, 0.0) for w in weights] for c in range(4)]


class Sums:
    def __init__(self):
        self.held = {}

    def add(self, offset, number, value):
        key = (offset, number)
        self.held[key] = value if key not in self.held else self.held[key] + value


def spread(blocks, weights, own, up, down):
    for c in range(4):
        centre, behind, ahead = weights[c]
        count = 1 << c
        per = 8 >> c
        for n in range(per):
            w = [blocks[k * per + n] for k in range(count)]
            moved = []
            for k in range(count):
                value = centre * w[k]
                if k > 0:
                    value += behind * w[k - 1]
                if k < count - 1:
                    value += ahead * w[k + 1]
                moved.append(value)
            above, below = behind * w[-1], ahead * w[0]
            line = moved + [above]
            own.add(0, n, moved[0])
            up.add(0, n, above)
            if count == 1:
                down.add(0, n, below)
            for k in range(1, count):
                s = k & -k
                own.add(k * 8 // count, n, line[k] - 0.5 * (line[k - s] + line[k + s]))
            level = 2
            while level <= count:
                up.add(8 // level, n, -0.5 * above)
                spill = -0.5 * moved[0]
                if level == count:
                    spill += below
                down.add(8 - 8 // level, n, spill)
                level *= 2


def contribute(first, weights_row, blocks_ref, at, own_ref, up_ref, down_ref):
    own, up, down = Sums(), Sums(), Sums()
    for grid in range(2):
        blocks = [blocks_ref[at, grid, 8 * n : 8 * n + 8, :] for n in range(8)]
        spread(blocks, weights_of(weights_row, grid), own, up, down)
    for offset, (start, count) in BLOCKS.items():
        for n in range(count):
            low = 8 * (start + n)
            targets = [(own_ref, low, own)]
            if offset in UP:
                targets.append((up_ref, low - UP_ROWS[0], up))
            if offset in DOWN:
                targets.append((down_ref, low - DOWN_ROWS[0], down))
            for ref, row, sums in targets:
                value = sums.held[offset, n]
                ref[row : row + 8, :] = value if first else ref[row : row + 8, :] + value


def weights_of(row, grid):
    return [
        [jnp.broadcast_to(row[:, 12 * grid + 3 * c + n : 12 * grid + 3 * c + n + 1], (8, 128)) for n in range(3)]
        for c in range(4)
    ]


def make_nodes(own_ref, up_ref, down_ref, halo, node_ref, next_ref, back_ref):
    prev_in, up_in, up_far, first_in, down_in, down_far = halo

    def block(ref, n):
        return ref[8 * n : 8 * n + 8, :]

    def held(offset, n):
        at = BLOCKS[offset][0] + n
        value = block(own_ref, at)
        if offset in UP:
            value += block(up_in, at)
        if offset in DOWN:
            value += block(down_in, at - 3)
        return value

    def before(offset, n):
        at = BLOCKS[offset][0] + n - 3
        value = block(prev_in, at) + block(down_ref, at)
        return value + block(up_far, at) if offset in (0, 4) else value

    for n in range(8):
        node = {0: held(0, n), 8: block(first_in, n) + block(up_ref, 3 + n) + block(down_far, n)}
        last = before(0, n)
        back_ref[0, n] = last
        next_ref[n] = node[8]
        node_ref[0, n] = node[0]
        for c in range(1, 4):
            if n >= 8 >> c:
                break
            s = 8 >> c
            for k in range(1, 1 << c, 2):
                node[k * s] = held(k * s, n) + 0.5 * (node[k * s - s] + node[k * s + s])
                node_ref[k * s, n] = node[k * s]
            last = before(8 - s, n) + 0.5 * (last + node[0])
            back_ref[c, n] = last


def interpolate(weights_row, node_ref, next_ref, back_ref, g_ref, at):
    weights = [weights_of(weights_row, grid) for grid in range(2)]
    sums = [Sums(), Sums()]
    for c in range(4):
        per = 8 >> c
        count = 1 << c
        for n in range(per):
            line = [back_ref[c, n]] + [node_ref[k * per, n] for k in range(count)] + [next_ref[n]]
            for k in range(count):
                for grid in range(2):
                    centre, behind, ahead = weights[grid][c]
                    sums[grid].add(
                        0, k * per + n, centre * line[k + 1] + behind * line[k] + ahead * line[k + 2]
                    )
    for grid in range(2):
        for n in range(8):
            g_ref[at, grid, 8 * n : 8 * n + 8, :] = sums[grid].held[0, n]


def kernel(
    nz, nd,
    lv_hbm, vel_hbm, rate_hbm, coef_hbm, v_hbm, s_hbm, out_ref,
    lv_ref, vel_ref, rate_ref, coef_ref, v_ref, s_ref, left_ref, right_ref, hat_ref,
    w_ref, w_in, row_ref, row_in, own_ref, up_ref, down_ref,
    prev_in, up_in, up_far, first_in, down_in, down_far,
    node_ref, next_ref, back_ref, g_ref, g_in,
    small_sem, load_sem, w_sem, row_sem, halo_sem, g_sem,
):
    z, d = lax.axis_index("grid"), lax.axis_index("dom")
    small = [
        pltpu.make_async_copy(source, target, small_sem.at[n])
        for n, (source, target) in enumerate(
            ((lv_hbm, lv_ref), (vel_hbm, vel_ref), (rate_hbm, rate_ref), (coef_hbm, coef_ref))
        )
    ]
    for copy in small:
        copy.start()
    loads = []
    for grid in range(2):
        for n, (source, target) in enumerate(((v_hbm, v_ref), (s_hbm, s_ref))):
            loads.append(pltpu.make_async_copy(source.at[grid], target.at[grid], load_sem.at[grid, n]))
            loads[-1].start()

    barrier = pltpu.get_barrier_semaphore()
    peers = [(lax.rem(z + n, nz), d) for n in range(1, nz)]
    peers += [(z, lax.rem(d + n, nd)) for n in (1, 2, nd - 1, nd - 2)]
    for peer in peers:
        pl.semaphore_signal(barrier, inc=1, device_id=peer, device_id_type=MESH)

    def remote(source, target, send, recv, peer):
        return pltpu.make_async_remote_copy(
            src_ref=source, dst_ref=target, send_sem=send, recv_sem=recv, device_id=peer, device_id_type=MESH
        )

    def near_first(i):
        return lax.rem(z + jnp.where(i % 2 == 0, 1 + i // 2, nz - (i + 1) // 2), nz)

    for copy in small:
        copy.wait()
    lane = lax.broadcasted_iota(jnp.int32, (1, 128), 1)
    row = jnp.zeros((1, 128), jnp.float32)
    for grid in range(2):
        for c, weights in enumerate(class_weights(grid, lv_ref, vel_ref)):
            for n, weight in enumerate(weights):
                row = jnp.where(lane == 12 * grid + 3 * c + n, weight, row)
    row_ref[...] = row
    for grid in range(2):
        @pl.loop(0, 8)
        def _(step):
            build_tables(grid, step, lv_ref, vel_ref, rate_ref, left_ref, hat_ref)

    for grid in range(2):
        loads[2 * grid].wait()
        loads[2 * grid + 1].wait()
        vh, vl = split(v_ref[grid])
        sh, sl = split(s_ref[grid])
        for slot, part in enumerate((vh, vl, vh, sh, sl)):
            right_ref[grid, :, slot * 256 : slot * 256 + 256] = part
        w = dot(left_ref[grid], right_ref[grid], ((1,), (1,))) * coef_ref[grid].astype(jnp.float32)
        for half in range(2):
            for quarter in range(QUARTERS):
                w_ref[half * QUARTERS + quarter, grid] = w[
                    quarter * 64 : quarter * 64 + 64, half * 128 : half * 128 + 128
                ]

    pl.semaphore_wait(barrier, len(peers))

    def w_copy(slot, target, peer):
        return remote(w_ref.at[peer], w_in.at[slot], w_sem.at[0, peer], w_sem.at[1, slot], (target, d))

    def row_copy(slot, target, peer):
        return remote(row_ref, row_in.at[slot], row_sem.at[0, peer], row_sem.at[1, slot], (target, d))

    @pl.loop(0, nz - 1)
    def _(i):
        peer = near_first(i)
        row_copy(z, peer, peer).start()
        w_copy(z, peer, peer).start()

    contribute(True, row_ref[...], w_ref, z, own_ref, up_ref, down_ref)

    @pl.loop(0, nz - 1)
    def _(i):
        peer = near_first(i)
        row_copy(peer, peer, peer).wait_recv()
        w_copy(peer, peer, peer).wait_recv()
        contribute(False, row_in[peer], w_in, peer, own_ref, up_ref, down_ref)

    def halo_copy(n, source, target, step):
        return remote(source, target, halo_sem.at[0, n], halo_sem.at[1, n], (z, lax.rem(d + nd + step, nd)))

    halos = [
        halo_copy(0, up_ref.at[24:120, :], up_far, 2),
        halo_copy(1, down_ref.at[0:64, :], down_far, -2),
        halo_copy(2, own_ref.at[24:144, :], prev_in, 1),
        halo_copy(3, own_ref.at[24:88, :], first_in, -1),
        halo_copy(4, up_ref, up_in, 1),
        halo_copy(5, down_ref, down_in, -1),
    ]
    for copy in halos:
        copy.start()
    for copy in halos:
        copy.wait_recv()
    make_nodes(
        own_ref, up_ref, down_ref, (prev_in, up_in, up_far, first_in, down_in, down_far),
        node_ref, next_ref, back_ref,
    )

    def g_copy(slot, target, peer):
        return remote(g_ref.at[peer], g_in.at[slot], g_sem.at[0, peer], g_sem.at[1, slot], (target, d))

    @pl.loop(0, nz)
    def _(peer):
        @pl.when(peer != z)
        def _():
            interpolate(row_in[peer], node_ref, next_ref, back_ref, g_ref, peer)
            g_copy(z, peer, peer).start()

    interpolate(row_ref[...], node_ref, next_ref, back_ref, g_in, z)

    for half in range(2):
        @pl.loop(half * QUARTERS, half * QUARTERS + QUARTERS)
        def _(peer):
            @pl.when(peer != z)
            def _():
                g_copy(peer, peer, peer).wait_recv()

        for grid in range(2):
            turned = jnp.transpose(
                jnp.concatenate([g_in[half * QUARTERS + n, grid] for n in range(QUARTERS)], axis=0)
            )
            high, low = split(turned)
            lanes = jnp.concatenate([high, low], axis=1)
            rows = slice(half * 128, half * 128 + 128)
            out_ref[grid, rows, :] = dot(lanes, hat_ref[grid], ((1,), (0,)))

    for copy in halos:
        copy.wait_send()

    @pl.loop(0, nz - 1)
    def _(i):
        peer = near_first(i)
        row_copy(z, peer, peer).wait_send()
        w_copy(z, peer, peer).wait_send()
        g_copy(z, peer, peer).wait_send()


def local(nz, nd, nodal_values, source_term, velocity, react_rate, levels, comb_coefs):
    f32, bf16 = jnp.float32, jnp.bfloat16
    hbm = pl.BlockSpec(memory_space=pl.ANY)
    sem = pltpu.SemaphoreType.DMA
    return pl.pallas_call(
        functools.partial(kernel, nz, nd),
        out_shape=jax.ShapeDtypeStruct((2, 256, 256), f32),
        in_specs=[hbm] * 6,
        out_specs=pl.BlockSpec(memory_space=pltpu.VMEM),
        scratch_shapes=[
            pltpu.SMEM((2, 2), jnp.int32),
            pltpu.SMEM((2, 2), f32),
            pltpu.SMEM((2,), f32),
            pltpu.SMEM((2,), jnp.int32),
            pltpu.VMEM((2, 256, 256), f32),
            pltpu.VMEM((2, 256, 256), f32),
            pltpu.VMEM((2, 256, KDIM), bf16),
            pltpu.VMEM((2, 256, KDIM), bf16),
            pltpu.VMEM((2, 512, 256), bf16),
            pltpu.VMEM((nz, 2, 64, 128), f32),
            pltpu.VMEM((nz, 2, 64, 128), f32),
            pltpu.VMEM((1, 128), f32),
            pltpu.VMEM((nz, 1, 128), f32),
            pltpu.VMEM((160, 128), f32),
            pltpu.VMEM((120, 128), f32),
            pltpu.VMEM((120, 128), f32),
            pltpu.VMEM((120, 128), f32),
            pltpu.VMEM((120, 128), f32),
            pltpu.VMEM((96, 128), f32),
            pltpu.VMEM((64, 128), f32),
            pltpu.VMEM((120, 128), f32),
            pltpu.VMEM((64, 128), f32),
            pltpu.VMEM((8, 8, 8, 128), f32),
            pltpu.VMEM((8, 8, 128), f32),
            pltpu.VMEM((4, 8, 8, 128), f32),
            pltpu.VMEM((nz, 2, 64, 128), f32),
            pltpu.VMEM((nz, 2, 64, 128), f32),
            sem((4,)),
            sem((2, 2)),
            sem((2, nz)),
            sem((2, nz)),
            sem((2, 6)),
            sem((2, nz)),
        ],
        compiler_params=pltpu.CompilerParams(collective_id=0, has_side_effects=True, vmem_limit_bytes=40 << 20),
    )(*[pltpu.with_memory_space_constraint(x, pltpu.HBM) for x in (levels, velocity, react_rate, comb_coefs, nodal_values, source_term)])


def solution(mesh):
    in_specs = (
        P("grid", None, "dom"),
        P("grid", None, "dom"),
        P("grid", None),
        P("grid"),
        P("grid", None),
        P("grid"),
    )
    body = functools.partial(local, mesh.shape["grid"], mesh.shape["dom"])
    return jax.shard_map(body, mesh=mesh, in_specs=in_specs, out_specs=P("grid", None, "dom"), check_vma=False)
```

```python
import functools

import jax
import jax.numpy as jnp
from jax import lax
from jax.experimental import pallas as pl
from jax.experimental.pallas import tpu as pltpu
from jax.sharding import PartitionSpec as P

TAU = 0.25
MESH = pl.DeviceIdType.MESH
BLOCKS = {2: (0, 2), 1: (2, 1), 0: (3, 8), 4: (11, 4), 6: (15, 2), 7: (17, 1), 3: (18, 1), 5: (19, 1)}
UP = (2, 1, 0, 4)
DOWN = (0, 4, 6, 7)
UP_ROWS = (0, 120)
DOWN_ROWS = (24, 120)
SUM_ROWS = 400
QUARTERS = 4
FAR = 1 << 20
KDIM = 1280


def dot(left, right, dims):
    return lax.dot_general(left, right, (dims, ((), ())), preferred_element_type=jnp.float32)


def split(value):
    high = value.astype(jnp.bfloat16)
    return high, (value - high.astype(jnp.float32)).astype(jnp.bfloat16)


def stencil(courant):
    square = courant * courant
    return 1.0 - square, 0.5 * (square + courant), 0.5 * (square - courant)


def build_tables(grid, step, lv_ref, vel_ref, rate_ref, left_ref, hat_ref):
    lx, m = lv_ref[grid, 0], lv_ref[grid, 1] - 5
    cols = jnp.left_shift(1, lx)
    gap = jnp.left_shift(1, 8 - lx)
    keep = 1.0 - TAU * rate_ref[grid]
    centre, behind, ahead = stencil(vel_ref[grid, 0] * cols.astype(jnp.float32) * (1.0 / 256.0))
    centre, behind, ahead = keep * centre, keep * behind, keep * ahead

    q = lax.broadcasted_iota(jnp.int32, (32, 128), 0) + step * 32
    quarter = jnp.right_shift(q, 6)
    t = q & 63
    row = jnp.right_shift(t, 6 - m)
    j = t & (jnp.right_shift(64, m) - 1)
    place = 64 * quarter + jnp.where(
        j < 8, 8 * j, jnp.where(j < 16, 8 * j - 60, jnp.where(j < 32, 4 * j - 62, 2 * j - 63))
    )
    reach = jnp.where(j < 8, FAR, jnp.where(j < 16, 4, jnp.where(j < 32, 2, 1)))
    slope = jnp.where(j < 8, 0.125, jnp.where(j < 16, 0.25, jnp.where(j < 32, 0.5, 1.0)))
    row_key = jnp.left_shift(jnp.where(j < jnp.right_shift(cols, 2), row, 1 << 12), 8)
    past = 256 - reach + gap
    past = jnp.where(past == 256, 0, past)
    rows = pl.ds(pl.multiple_of(step * 32, 32), 32)
    for half in range(2):
        p = lax.broadcasted_iota(jnp.int32, (1, 128), 1) + 128 * half
        at = jnp.left_shift(p & (cols - 1), 8 - lx)
        key = jnp.left_shift(jnp.right_shift(p, lx), 8)
        other = key ^ row_key
        apart = (at - place) & 255
        delta = apart | other

        def pick(target, weight):
            return jnp.where(delta == target, weight, 0.0)

        here, right, left = delta == 0, delta == reach, delta == 256 - reach
        tree = jnp.where(here, 1.0, 0.0) - jnp.where(right, 0.5, 0.0) - jnp.where(left, 0.5, 0.0)
        full = (
            centre * tree
            + behind * (pick(256 - gap, 1.0) - pick(reach - gap, 0.5) - pick(256 - reach - gap, 0.5))
            + ahead * (pick(gap, 1.0) - pick(reach + gap, 0.5) - pick(past, 0.5))
        )
        high, low = split(full)
        quart = (TAU * tree).astype(jnp.bfloat16)
        for slot, table in enumerate((high, high, low, quart, quart)):
            left_ref[grid, rows, slot * 256 + half * 128 : slot * 256 + half * 128 + 128] = table
        near = jnp.minimum(apart, 256 - apart).astype(jnp.float32)
        hat = jnp.where(other == 0, jnp.maximum(0.0, 1.0 - near * slope), 0.0).astype(jnp.bfloat16)
        lanes = slice(half * 128, half * 128 + 128)
        hat_ref[grid, rows, lanes] = hat
        hat_ref[grid, pl.ds(pl.multiple_of(256 + step * 32, 32), 32), lanes] = hat


def class_weights(grid, lv_ref, vel_ref):
    m = lv_ref[grid, 1] - 5
    rows = jnp.left_shift(1, m).astype(jnp.float32)
    weights = stencil(vel_ref[grid, 1] * rows * 0.125)
    return [[jnp.where(m == c, w, 0.0) for w in weights] for c in range(4)]


class Sums:
    def __init__(self):
        self.held = {}

    def add(self, offset, number, value):
        key = (offset, number)
        self.held[key] = value if key not in self.held else self.held[key] + value


def spread(blocks, weights, own, up, down):
    for c in range(4):
        centre, behind, ahead = weights[c]
        count = 1 << c
        per = 8 >> c
        for n in range(per):
            w = [blocks[k * per + n] for k in range(count)]
            moved = []
            for k in range(count):
                value = centre * w[k]
                if k > 0:
                    value += behind * w[k - 1]
                if k < count - 1:
                    value += ahead * w[k + 1]
                moved.append(value)
            above, below = behind * w[-1], ahead * w[0]
            line = moved + [above]
            own.add(0, n, moved[0])
            up.add(0, n, above)
            if count == 1:
                down.add(0, n, below)
            for k in range(1, count):
                s = k & -k
                own.add(k * 8 // count, n, line[k] - 0.5 * (line[k - s] + line[k + s]))
            level = 2
            while level <= count:
                up.add(8 // level, n, -0.5 * above)
                spill = -0.5 * moved[0]
                if level == count:
                    spill += below
                down.add(8 - 8 // level, n, spill)
                level *= 2


def own_row(low):
    return 360 + low if low < 24 else 96 + low if low < 144 else 240 + low


def contribute(first, weights_row, blocks_ref, at, sums_ref):
    own, up, down = Sums(), Sums(), Sums()
    for grid in range(2):
        blocks = [blocks_ref[at, grid, 8 * n : 8 * n + 8, :] for n in range(8)]
        spread(blocks, weights_of(weights_row, grid), own, up, down)
    for offset, (start, count) in BLOCKS.items():
        for n in range(count):
            low = 8 * (start + n)
            targets = [(own_row(low), own)]
            if offset in UP:
                targets.append((240 + low - UP_ROWS[0], up))
            if offset in DOWN:
                targets.append((low - DOWN_ROWS[0], down))
            for row, sums in targets:
                value = sums.held[offset, n]
                sums_ref[row : row + 8, :] = value if first else sums_ref[row : row + 8, :] + value


def weights_of(row, grid):
    return [
        [jnp.broadcast_to(row[:, 12 * grid + 3 * c + n : 12 * grid + 3 * c + n + 1], (8, 128)) for n in range(3)]
        for c in range(4)
    ]


def make_nodes(sums_ref, halo, node_ref, next_ref, back_ref):
    after_in, before_in, up_far, down_far = halo

    def block(ref, n, start=0):
        return ref[start + 8 * n : start + 8 * n + 8, :]

    def held(offset, n):
        at = BLOCKS[offset][0] + n
        value = block(sums_ref, 0, own_row(8 * at))
        if offset in UP:
            value += block(after_in, at, 120)
        if offset in DOWN:
            value += block(before_in, at - 3)
        return value

    def before(offset, n):
        at = BLOCKS[offset][0] + n - 3
        value = block(after_in, at) + block(sums_ref, at)
        return value + block(up_far, at) if offset in (0, 4) else value

    for n in range(8):
        node = {0: held(0, n), 8: block(before_in, n, 120) + block(sums_ref, 3 + n, 240) + block(down_far, n)}
        last = before(0, n)
        back_ref[0, n] = last
        next_ref[n] = node[8]
        node_ref[0, n] = node[0]
        for c in range(1, 4):
            if n >= 8 >> c:
                break
            s = 8 >> c
            for k in range(1, 1 << c, 2):
                node[k * s] = held(k * s, n) + 0.5 * (node[k * s - s] + node[k * s + s])
                node_ref[k * s, n] = node[k * s]
            last = before(8 - s, n) + 0.5 * (last + node[0])
            back_ref[c, n] = last


def interpolate(weights_row, node_ref, next_ref, back_ref, g_ref, at):
    weights = [weights_of(weights_row, grid) for grid in range(2)]
    sums = [Sums(), Sums()]
    for c in range(4):
        per = 8 >> c
        count = 1 << c
        for n in range(per):
            line = [back_ref[c, n]] + [node_ref[k * per, n] for k in range(count)] + [next_ref[n]]
            for k in range(count):
                for grid in range(2):
                    centre, behind, ahead = weights[grid][c]
                    sums[grid].add(
                        0, k * per + n, centre * line[k + 1] + behind * line[k] + ahead * line[k + 2]
                    )
    for grid in range(2):
        for n in range(8):
            g_ref[at, grid, 8 * n : 8 * n + 8, :] = sums[grid].held[0, n]


def kernel(
    nz, nd,
    lv_hbm, vel_hbm, rate_hbm, coef_hbm, v_hbm, s_hbm, out_ref,
    lv_ref, vel_ref, rate_ref, coef_ref, v_ref, s_ref, left_ref, right_ref, hat_ref,
    w_ref, w_in, row_ref, row_in, sums_ref,
    after_in, before_in, up_far, down_far,
    node_ref, next_ref, back_ref, g_ref, g_in,
    small_sem, load_sem, w_sem, row_sem, halo_sem, g_sem,
):
    z, d = lax.axis_index("grid"), lax.axis_index("dom")
    small = [
        pltpu.make_async_copy(source, target, small_sem.at[n])
        for n, (source, target) in enumerate(
            ((lv_hbm, lv_ref), (vel_hbm, vel_ref), (rate_hbm, rate_ref), (coef_hbm, coef_ref))
        )
    ]
    for copy in small:
        copy.start()
    loads = []
    for grid in range(2):
        for n, (source, target) in enumerate(((v_hbm, v_ref), (s_hbm, s_ref))):
            loads.append(pltpu.make_async_copy(source.at[grid], target.at[grid], load_sem.at[grid, n]))
            loads[-1].start()

    barrier = pltpu.get_barrier_semaphore()
    peers = [(lax.rem(z + n, nz), d) for n in range(1, nz)]
    peers += [(z, lax.rem(d + n, nd)) for n in (1, 2, nd - 1, nd - 2)]
    for peer in peers:
        pl.semaphore_signal(barrier, inc=1, device_id=peer, device_id_type=MESH)

    def remote(source, target, send, recv, peer):
        return pltpu.make_async_remote_copy(
            src_ref=source, dst_ref=target, send_sem=send, recv_sem=recv, device_id=peer, device_id_type=MESH
        )

    def near_first(i):
        return lax.rem(z + jnp.where(i % 2 == 0, 1 + i // 2, nz - (i + 1) // 2), nz)

    for copy in small:
        copy.wait()
    lane = lax.broadcasted_iota(jnp.int32, (1, 128), 1)
    row = jnp.zeros((1, 128), jnp.float32)
    for grid in range(2):
        for c, weights in enumerate(class_weights(grid, lv_ref, vel_ref)):
            for n, weight in enumerate(weights):
                row = jnp.where(lane == 12 * grid + 3 * c + n, weight, row)
    row_ref[...] = row
    for grid in range(2):
        @pl.loop(0, 8)
        def _(step):
            build_tables(grid, step, lv_ref, vel_ref, rate_ref, left_ref, hat_ref)

    for grid in range(2):
        loads[2 * grid].wait()
        loads[2 * grid + 1].wait()
        vh, vl = split(v_ref[grid])
        sh, sl = split(s_ref[grid])
        for slot, part in enumerate((vh, vl, vh, sh, sl)):
            right_ref[grid, :, slot * 256 : slot * 256 + 256] = part
        w = dot(left_ref[grid], right_ref[grid], ((1,), (1,))) * coef_ref[grid].astype(jnp.float32)
        for half in range(2):
            for quarter in range(QUARTERS):
                w_ref[half * QUARTERS + quarter, grid] = w[
                    quarter * 64 : quarter * 64 + 64, half * 128 : half * 128 + 128
                ]

    pl.semaphore_wait(barrier, len(peers))

    def w_copy(slot, target, peer):
        return remote(w_ref.at[peer], w_in.at[slot], w_sem.at[0, peer], w_sem.at[1, slot], (target, d))

    def row_copy(slot, target, peer):
        return remote(row_ref, row_in.at[slot], row_sem.at[0, peer], row_sem.at[1, slot], (target, d))

    @pl.loop(0, nz - 1)
    def _(i):
        peer = near_first(i)
        row_copy(z, peer, peer).start()
        w_copy(z, peer, peer).start()

    contribute(True, row_ref[...], w_ref, z, sums_ref)

    @pl.loop(0, nz - 1)
    def _(i):
        peer = near_first(i)
        row_copy(peer, peer, peer).wait_recv()
        w_copy(peer, peer, peer).wait_recv()
        contribute(False, row_in[peer], w_in, peer, sums_ref)

    def halo_copy(n, source, target, step):
        return remote(source, target, halo_sem.at[0, n], halo_sem.at[1, n], (z, lax.rem(d + nd + step, nd)))

    halos = [
        halo_copy(0, sums_ref.at[264:360, :], up_far, 2),
        halo_copy(1, sums_ref.at[0:64, :], down_far, -2),
        halo_copy(2, sums_ref.at[120:360, :], after_in, 1),
        halo_copy(3, sums_ref.at[0:184, :], before_in, -1),
    ]
    for copy in halos:
        copy.start()
    for copy in halos:
        copy.wait_recv()
    make_nodes(
        sums_ref, (after_in, before_in, up_far, down_far), node_ref, next_ref, back_ref,
    )

    def g_copy(slot, target, peer):
        return remote(g_ref.at[peer], g_in.at[slot], g_sem.at[0, peer], g_sem.at[1, slot], (target, d))

    @pl.loop(0, nz)
    def _(i):
        peer = jnp.where(i % 4 == 1, i + 1, jnp.where(i % 4 == 2, i - 1, i))

        @pl.when(peer != z)
        def _():
            interpolate(row_in[peer], node_ref, next_ref, back_ref, g_ref, peer)
            g_copy(z, peer, peer).start()

    interpolate(row_ref[...], node_ref, next_ref, back_ref, g_in, z)

    for half in range(2):
        @pl.loop(half * QUARTERS, half * QUARTERS + QUARTERS)
        def _(peer):
            @pl.when(peer != z)
            def _():
                g_copy(peer, peer, peer).wait_recv()

        for grid in range(2):
            turned = jnp.transpose(
                jnp.concatenate([g_in[half * QUARTERS + n, grid] for n in range(QUARTERS)], axis=0)
            )
            high, low = split(turned)
            lanes = jnp.concatenate([high, low], axis=1)
            rows = slice(half * 128, half * 128 + 128)
            out_ref[grid, rows, :] = dot(lanes, hat_ref[grid], ((1,), (0,)))

    for copy in halos:
        copy.wait_send()

    @pl.loop(0, nz - 1)
    def _(i):
        peer = near_first(i)
        row_copy(z, peer, peer).wait_send()
        w_copy(z, peer, peer).wait_send()
        g_copy(z, peer, peer).wait_send()


def local(nz, nd, nodal_values, source_term, velocity, react_rate, levels, comb_coefs):
    f32, bf16 = jnp.float32, jnp.bfloat16
    hbm = pl.BlockSpec(memory_space=pl.ANY)
    sem = pltpu.SemaphoreType.DMA
    return pl.pallas_call(
        functools.partial(kernel, nz, nd),
        out_shape=jax.ShapeDtypeStruct((2, 256, 256), f32),
        in_specs=[hbm] * 6,
        out_specs=pl.BlockSpec(memory_space=pltpu.VMEM),
        scratch_shapes=[
            pltpu.SMEM((2, 2), jnp.int32),
            pltpu.SMEM((2, 2), f32),
            pltpu.SMEM((2,), f32),
            pltpu.SMEM((2,), jnp.int32),
            pltpu.VMEM((2, 256, 256), f32),
            pltpu.VMEM((2, 256, 256), f32),
            pltpu.VMEM((2, 256, KDIM), bf16),
            pltpu.VMEM((2, 256, KDIM), bf16),
            pltpu.VMEM((2, 512, 256), bf16),
            pltpu.VMEM((nz, 2, 64, 128), f32),
            pltpu.VMEM((nz, 2, 64, 128), f32),
            pltpu.VMEM((1, 128), f32),
            pltpu.VMEM((nz, 1, 128), f32),
            pltpu.VMEM((SUM_ROWS, 128), f32),
            pltpu.VMEM((240, 128), f32),
            pltpu.VMEM((184, 128), f32),
            pltpu.VMEM((96, 128), f32),
            pltpu.VMEM((64, 128), f32),
            pltpu.VMEM((8, 8, 8, 128), f32),
            pltpu.VMEM((8, 8, 128), f32),
            pltpu.VMEM((4, 8, 8, 128), f32),
            pltpu.VMEM((nz, 2, 64, 128), f32),
            pltpu.VMEM((nz, 2, 64, 128), f32),
            sem((4,)),
            sem((2, 2)),
            sem((2, nz)),
            sem((2, nz)),
            sem((2, 4)),
            sem((2, nz)),
        ],
        compiler_params=pltpu.CompilerParams(collective_id=0, has_side_effects=True, vmem_limit_bytes=40 << 20),
    )(*[pltpu.with_memory_space_constraint(x, pltpu.HBM) for x in (levels, velocity, react_rate, comb_coefs, nodal_values, source_term)])


def solution(mesh):
    in_specs = (
        P("grid", None, "dom"),
        P("grid", None, "dom"),
        P("grid", None),
        P("grid"),
        P("grid", None),
        P("grid"),
    )
    body = functools.partial(local, mesh.shape["grid"], mesh.shape["dom"])
    return jax.shard_map(body, mesh=mesh, in_specs=in_specs, out_specs=P("grid", None, "dom"), check_vma=False)
```

```python
import functools

import jax
import jax.numpy as jnp
from jax import lax
from jax.experimental import pallas as pl
from jax.experimental.pallas import tpu as pltpu
from jax.sharding import PartitionSpec as P

TAU = 0.25
MESH = pl.DeviceIdType.MESH
BLOCKS = {2: (0, 2), 1: (2, 1), 0: (3, 8), 4: (11, 4), 6: (15, 2), 7: (17, 1), 3: (18, 1), 5: (19, 1)}
UP = (2, 1, 0, 4)
DOWN = (0, 4, 6, 7)
UP_ROWS = (0, 120)
DOWN_ROWS = (24, 120)
SUM_ROWS = 400
QUARTERS = 4
FAR = 1 << 20
KDIM = 1280


def dot(left, right, dims):
    return lax.dot_general(left, right, (dims, ((), ())), preferred_element_type=jnp.float32)


def split(value):
    high = value.astype(jnp.bfloat16)
    return high, (value - high.astype(jnp.float32)).astype(jnp.bfloat16)


def stencil(courant):
    square = courant * courant
    return 1.0 - square, 0.5 * (square + courant), 0.5 * (square - courant)


def build_tables(grid, step, lv_ref, vel_ref, rate_ref, left_ref, hat_ref):
    lx, m = lv_ref[grid, 0], lv_ref[grid, 1] - 5
    cols = jnp.left_shift(1, lx)
    gap = jnp.left_shift(1, 8 - lx)
    keep = 1.0 - TAU * rate_ref[grid]
    centre, behind, ahead = stencil(vel_ref[grid, 0] * cols.astype(jnp.float32) * (1.0 / 256.0))
    centre, behind, ahead = keep * centre, keep * behind, keep * ahead

    q = lax.broadcasted_iota(jnp.int32, (32, 128), 0) + step * 32
    quarter = jnp.right_shift(q, 6)
    t = q & 63
    row = jnp.right_shift(t, 6 - m)
    j = t & (jnp.right_shift(64, m) - 1)
    place = 64 * quarter + jnp.where(
        j < 8, 8 * j, jnp.where(j < 16, 8 * j - 60, jnp.where(j < 32, 4 * j - 62, 2 * j - 63))
    )
    reach = jnp.where(j < 8, FAR, jnp.where(j < 16, 4, jnp.where(j < 32, 2, 1)))
    slope = jnp.where(j < 8, 0.125, jnp.where(j < 16, 0.25, jnp.where(j < 32, 0.5, 1.0)))
    row_key = jnp.left_shift(jnp.where(j < jnp.right_shift(cols, 2), row, 1 << 12), 8)
    past = 256 - reach + gap
    past = jnp.where(past == 256, 0, past)
    rows = pl.ds(pl.multiple_of(step * 32, 32), 32)
    for half in range(2):
        p = lax.broadcasted_iota(jnp.int32, (1, 128), 1) + 128 * half
        at = jnp.left_shift(p & (cols - 1), 8 - lx)
        key = jnp.left_shift(jnp.right_shift(p, lx), 8)
        other = key ^ row_key
        apart = (at - place) & 255
        delta = apart | other

        def pick(target, weight):
            return jnp.where(delta == target, weight, 0.0)

        here, right, left = delta == 0, delta == reach, delta == 256 - reach
        tree = jnp.where(here, 1.0, 0.0) - jnp.where(right, 0.5, 0.0) - jnp.where(left, 0.5, 0.0)
        full = (
            centre * tree
            + behind * (pick(256 - gap, 1.0) - pick(reach - gap, 0.5) - pick(256 - reach - gap, 0.5))
            + ahead * (pick(gap, 1.0) - pick(reach + gap, 0.5) - pick(past, 0.5))
        )
        high, low = split(full)
        quart = (TAU * tree).astype(jnp.bfloat16)
        for slot, table in enumerate((high, high, low, quart, quart)):
            left_ref[grid, rows, slot * 256 + half * 128 : slot * 256 + half * 128 + 128] = table
        near = jnp.minimum(apart, 256 - apart).astype(jnp.float32)
        hat = jnp.where(other == 0, jnp.maximum(0.0, 1.0 - near * slope), 0.0).astype(jnp.bfloat16)
        lanes = slice(half * 128, half * 128 + 128)
        hat_ref[grid, rows, lanes] = hat
        hat_ref[grid, pl.ds(pl.multiple_of(256 + step * 32, 32), 32), lanes] = hat


def class_weights(grid, lv_ref, vel_ref):
    m = lv_ref[grid, 1] - 5
    rows = jnp.left_shift(1, m).astype(jnp.float32)
    weights = stencil(vel_ref[grid, 1] * rows * 0.125)
    return [[jnp.where(m == c, w, 0.0) for w in weights] for c in range(4)]


class Sums:
    def __init__(self):
        self.held = {}

    def add(self, offset, number, value):
        key = (offset, number)
        self.held[key] = value if key not in self.held else self.held[key] + value


def spread(blocks, weights, own, up, down):
    for c in range(4):
        centre, behind, ahead = weights[c]
        count = 1 << c
        per = 8 >> c
        for n in range(per):
            w = [blocks[k * per + n] for k in range(count)]
            moved = []
            for k in range(count):
                value = centre * w[k]
                if k > 0:
                    value += behind * w[k - 1]
                if k < count - 1:
                    value += ahead * w[k + 1]
                moved.append(value)
            above, below = behind * w[-1], ahead * w[0]
            line = moved + [above]
            own.add(0, n, moved[0])
            up.add(0, n, above)
            if count == 1:
                down.add(0, n, below)
            for k in range(1, count):
                s = k & -k
                own.add(k * 8 // count, n, line[k] - 0.5 * (line[k - s] + line[k + s]))
            level = 2
            while level <= count:
                up.add(8 // level, n, -0.5 * above)
                spill = -0.5 * moved[0]
                if level == count:
                    spill += below
                down.add(8 - 8 // level, n, spill)
                level *= 2


def own_row(low):
    return 360 + low if low < 24 else 96 + low if low < 144 else 240 + low


def contribute(first, weights_row, blocks_ref, at, sums_ref):
    own, up, down = Sums(), Sums(), Sums()
    for grid in range(2):
        blocks = [blocks_ref[at, grid, 8 * n : 8 * n + 8, :] for n in range(8)]
        spread(blocks, weights_of(weights_row, grid), own, up, down)
    for offset, (start, count) in BLOCKS.items():
        for n in range(count):
            low = 8 * (start + n)
            targets = [(own_row(low), own)]
            if offset in UP:
                targets.append((240 + low - UP_ROWS[0], up))
            if offset in DOWN:
                targets.append((low - DOWN_ROWS[0], down))
            for row, sums in targets:
                value = sums.held[offset, n]
                sums_ref[row : row + 8, :] = value if first else sums_ref[row : row + 8, :] + value


def weights_of(row, grid):
    return [
        [jnp.broadcast_to(row[:, 12 * grid + 3 * c + n : 12 * grid + 3 * c + n + 1], (8, 128)) for n in range(3)]
        for c in range(4)
    ]


def make_nodes(sums_ref, halo, node_ref, next_ref, back_ref):
    after_in, before_in, up_far, down_far = halo

    def block(ref, n, start=0):
        return ref[start + 8 * n : start + 8 * n + 8, :]

    def held(offset, n):
        at = BLOCKS[offset][0] + n
        value = block(sums_ref, 0, own_row(8 * at))
        if offset in UP:
            value += block(after_in, at, 120)
        if offset in DOWN:
            value += block(before_in, at - 3)
        return value

    def before(offset, n):
        at = BLOCKS[offset][0] + n - 3
        value = block(after_in, at) + block(sums_ref, at)
        return value + block(up_far, at) if offset in (0, 4) else value

    for n in range(8):
        node = {0: held(0, n), 8: block(before_in, n, 120) + block(sums_ref, 3 + n, 240) + block(down_far, n)}
        last = before(0, n)
        back_ref[0, n] = last
        next_ref[n] = node[8]
        node_ref[0, n] = node[0]
        for c in range(1, 4):
            if n >= 8 >> c:
                break
            s = 8 >> c
            for k in range(1, 1 << c, 2):
                node[k * s] = held(k * s, n) + 0.5 * (node[k * s - s] + node[k * s + s])
                node_ref[k * s, n] = node[k * s]
            last = before(8 - s, n) + 0.5 * (last + node[0])
            back_ref[c, n] = last


def interpolate(weights_row, node_ref, next_ref, back_ref, g_ref, at):
    weights = [weights_of(weights_row, grid) for grid in range(2)]
    sums = [Sums(), Sums()]
    for c in range(4):
        per = 8 >> c
        count = 1 << c
        for n in range(per):
            line = [back_ref[c, n]] + [node_ref[k * per, n] for k in range(count)] + [next_ref[n]]
            for k in range(count):
                for grid in range(2):
                    centre, behind, ahead = weights[grid][c]
                    sums[grid].add(
                        0, k * per + n, centre * line[k + 1] + behind * line[k] + ahead * line[k + 2]
                    )
    for grid in range(2):
        for n in range(8):
            g_ref[at, grid, 8 * n : 8 * n + 8, :] = sums[grid].held[0, n]


def kernel(
    nz, nd,
    lv_hbm, vel_hbm, rate_hbm, coef_hbm, v_hbm, s_hbm, out_ref,
    lv_ref, vel_ref, rate_ref, coef_ref, v_ref, s_ref, left_ref, right_ref, hat_ref,
    w_ref, w_in, row_ref, row_in, sums_ref,
    after_in, before_in, up_far, down_far,
    node_ref, next_ref, back_ref, g_ref, g_in,
    small_sem, load_sem, w_sem, row_sem, halo_sem, g_sem,
):
    z, d = lax.axis_index("grid"), lax.axis_index("dom")
    small = [
        pltpu.make_async_copy(source, target, small_sem.at[n])
        for n, (source, target) in enumerate(
            ((lv_hbm, lv_ref), (vel_hbm, vel_ref), (rate_hbm, rate_ref), (coef_hbm, coef_ref))
        )
    ]
    for copy in small:
        copy.start()
    loads = []
    for grid in range(2):
        for n, (source, target) in enumerate(((v_hbm, v_ref), (s_hbm, s_ref))):
            loads.append(pltpu.make_async_copy(source.at[grid], target.at[grid], load_sem.at[grid, n]))
            loads[-1].start()

    barrier = pltpu.get_barrier_semaphore()
    peers = [(lax.rem(z + n, nz), d) for n in range(1, nz)]
    peers += [(z, lax.rem(d + n, nd)) for n in (1, 2, nd - 1, nd - 2)]
    for peer in peers:
        pl.semaphore_signal(barrier, inc=1, device_id=peer, device_id_type=MESH)

    def remote(source, target, send, recv, peer):
        return pltpu.make_async_remote_copy(
            src_ref=source, dst_ref=target, send_sem=send, recv_sem=recv, device_id=peer, device_id_type=MESH
        )

    def near_first(i):
        return lax.rem(z + jnp.where(i % 2 == 0, 1 + i // 2, nz - (i + 1) // 2), nz)

    for copy in small:
        copy.wait()
    lane = lax.broadcasted_iota(jnp.int32, (1, 128), 1)
    row = jnp.zeros((1, 128), jnp.float32)
    for grid in range(2):
        for c, weights in enumerate(class_weights(grid, lv_ref, vel_ref)):
            for n, weight in enumerate(weights):
                row = jnp.where(lane == 12 * grid + 3 * c + n, weight, row)
    row_ref[...] = row
    for grid in range(2):
        @pl.loop(0, 8)
        def _(step):
            build_tables(grid, step, lv_ref, vel_ref, rate_ref, left_ref, hat_ref)

    for grid in range(2):
        loads[2 * grid].wait()
        loads[2 * grid + 1].wait()
        vh, vl = split(v_ref[grid])
        sh, sl = split(s_ref[grid])
        for slot, part in enumerate((vh, vl, vh, sh, sl)):
            right_ref[grid, :, slot * 256 : slot * 256 + 256] = part
        w = dot(left_ref[grid], right_ref[grid], ((1,), (1,))) * coef_ref[grid].astype(jnp.float32)
        for half in range(2):
            for quarter in range(QUARTERS):
                w_ref[half * QUARTERS + quarter, grid] = w[
                    quarter * 64 : quarter * 64 + 64, half * 128 : half * 128 + 128
                ]

    pl.semaphore_wait(barrier, len(peers))

    def w_copy(slot, target, peer):
        return remote(w_ref.at[peer], w_in.at[slot], w_sem.at[0, peer], w_sem.at[1, slot], (target, d))

    def row_copy(slot, target, peer):
        return remote(row_ref, row_in.at[slot], row_sem.at[0, peer], row_sem.at[1, slot], (target, d))

    @pl.loop(0, nz - 1)
    def _(i):
        peer = near_first(i)
        row_copy(z, peer, peer).start()
        w_copy(z, peer, peer).start()

    contribute(True, row_ref[...], w_ref, z, sums_ref)

    @pl.loop(0, nz - 1)
    def _(i):
        peer = near_first(i)
        row_copy(peer, peer, peer).wait_recv()
        w_copy(peer, peer, peer).wait_recv()
        contribute(False, row_in[peer], w_in, peer, sums_ref)

    def halo_copy(n, source, target, step):
        return remote(source, target, halo_sem.at[0, n], halo_sem.at[1, n], (z, lax.rem(d + nd + step, nd)))

    halos = [
        halo_copy(0, sums_ref.at[264:360, :], up_far, 2),
        halo_copy(1, sums_ref.at[0:64, :], down_far, -2),
        halo_copy(2, sums_ref.at[120:360, :], after_in, 1),
        halo_copy(3, sums_ref.at[0:184, :], before_in, -1),
    ]
    for copy in halos:
        copy.start()
    for copy in halos:
        copy.wait_recv()
    make_nodes(
        sums_ref, (after_in, before_in, up_far, down_far), node_ref, next_ref, back_ref,
    )

    def g_copy(slot, target, peer):
        return remote(g_ref.at[peer], g_in.at[slot], g_sem.at[0, peer], g_sem.at[1, slot], (target, d))

    @pl.loop(0, nz)
    def _(i):
        peer = jnp.where(i < 3, lax.rem(i + 2, 3), jnp.where(i == 5, 6, jnp.where(i == 6, 5, i)))

        @pl.when(peer != z)
        def _():
            interpolate(row_in[peer], node_ref, next_ref, back_ref, g_ref, peer)
            g_copy(z, peer, peer).start()

    interpolate(row_ref[...], node_ref, next_ref, back_ref, g_in, z)

    for half in range(2):
        @pl.loop(half * QUARTERS, half * QUARTERS + QUARTERS)
        def _(peer):
            @pl.when(peer != z)
            def _():
                g_copy(peer, peer, peer).wait_recv()

        for grid in range(2):
            turned = jnp.transpose(
                jnp.concatenate([g_in[half * QUARTERS + n, grid] for n in range(QUARTERS)], axis=0)
            )
            high, low = split(turned)
            lanes = jnp.concatenate([high, low], axis=1)
            rows = slice(half * 128, half * 128 + 128)
            out_ref[grid, rows, :] = dot(lanes, hat_ref[grid], ((1,), (0,)))

    for copy in halos:
        copy.wait_send()

    @pl.loop(0, nz - 1)
    def _(i):
        peer = near_first(i)
        row_copy(z, peer, peer).wait_send()
        w_copy(z, peer, peer).wait_send()
        g_copy(z, peer, peer).wait_send()


def local(nz, nd, nodal_values, source_term, velocity, react_rate, levels, comb_coefs):
    f32, bf16 = jnp.float32, jnp.bfloat16
    hbm = pl.BlockSpec(memory_space=pl.ANY)
    sem = pltpu.SemaphoreType.DMA
    return pl.pallas_call(
        functools.partial(kernel, nz, nd),
        out_shape=jax.ShapeDtypeStruct((2, 256, 256), f32),
        in_specs=[hbm] * 6,
        out_specs=pl.BlockSpec(memory_space=pltpu.VMEM),
        scratch_shapes=[
            pltpu.SMEM((2, 2), jnp.int32),
            pltpu.SMEM((2, 2), f32),
            pltpu.SMEM((2,), f32),
            pltpu.SMEM((2,), jnp.int32),
            pltpu.VMEM((2, 256, 256), f32),
            pltpu.VMEM((2, 256, 256), f32),
            pltpu.VMEM((2, 256, KDIM), bf16),
            pltpu.VMEM((2, 256, KDIM), bf16),
            pltpu.VMEM((2, 512, 256), bf16),
            pltpu.VMEM((nz, 2, 64, 128), f32),
            pltpu.VMEM((nz, 2, 64, 128), f32),
            pltpu.VMEM((1, 128), f32),
            pltpu.VMEM((nz, 1, 128), f32),
            pltpu.VMEM((SUM_ROWS, 128), f32),
            pltpu.VMEM((240, 128), f32),
            pltpu.VMEM((184, 128), f32),
            pltpu.VMEM((96, 128), f32),
            pltpu.VMEM((64, 128), f32),
            pltpu.VMEM((8, 8, 8, 128), f32),
            pltpu.VMEM((8, 8, 128), f32),
            pltpu.VMEM((4, 8, 8, 128), f32),
            pltpu.VMEM((nz, 2, 64, 128), f32),
            pltpu.VMEM((nz, 2, 64, 128), f32),
            sem((4,)),
            sem((2, 2)),
            sem((2, nz)),
            sem((2, nz)),
            sem((2, 4)),
            sem((2, nz)),
        ],
        compiler_params=pltpu.CompilerParams(collective_id=0, has_side_effects=True, vmem_limit_bytes=40 << 20),
    )(*[pltpu.with_memory_space_constraint(x, pltpu.HBM) for x in (levels, velocity, react_rate, comb_coefs, nodal_values, source_term)])


def solution(mesh):
    in_specs = (
        P("grid", None, "dom"),
        P("grid", None, "dom"),
        P("grid", None),
        P("grid"),
        P("grid", None),
        P("grid"),
    )
    body = functools.partial(local, mesh.shape["grid"], mesh.shape["dom"])
    return jax.shard_map(body, mesh=mesh, in_specs=in_specs, out_specs=P("grid", None, "dom"), check_vma=False)
```

```python
import functools

import jax
import jax.numpy as jnp
from jax import lax
from jax.experimental import pallas as pl
from jax.experimental.pallas import tpu as pltpu
from jax.sharding import PartitionSpec as P

TAU = 0.25
MESH = pl.DeviceIdType.MESH
BLOCKS = {2: (0, 2), 1: (2, 1), 0: (3, 8), 4: (11, 4), 6: (15, 2), 7: (17, 1), 3: (18, 1), 5: (19, 1)}
UP = (2, 1, 0, 4)
DOWN = (0, 4, 6, 7)
UP_ROWS = (0, 120)
DOWN_ROWS = (24, 120)
SUM_ROWS = 400
QUARTERS = 4
FAR = 1 << 20
KDIM = 1280


def dot(left, right, dims):
    return lax.dot_general(left, right, (dims, ((), ())), preferred_element_type=jnp.float32)


def split(value):
    high = value.astype(jnp.bfloat16)
    return high, (value - high.astype(jnp.float32)).astype(jnp.bfloat16)


def stencil(courant):
    square = courant * courant
    return 1.0 - square, 0.5 * (square + courant), 0.5 * (square - courant)


def build_tables(grid, step, lv_ref, vel_ref, rate_ref, left_ref, hat_ref):
    lx, m = lv_ref[grid, 0], lv_ref[grid, 1] - 5
    cols = jnp.left_shift(1, lx)
    gap = jnp.left_shift(1, 8 - lx)
    keep = 1.0 - TAU * rate_ref[grid]
    centre, behind, ahead = stencil(vel_ref[grid, 0] * cols.astype(jnp.float32) * (1.0 / 256.0))
    centre, behind, ahead = keep * centre, keep * behind, keep * ahead

    q = lax.broadcasted_iota(jnp.int32, (32, 128), 0) + step * 32
    quarter = jnp.right_shift(q, 6)
    t = q & 63
    row = jnp.right_shift(t, 6 - m)
    j = t & (jnp.right_shift(64, m) - 1)
    place = 64 * quarter + jnp.where(
        j < 8, 8 * j, jnp.where(j < 16, 8 * j - 60, jnp.where(j < 32, 4 * j - 62, 2 * j - 63))
    )
    reach = jnp.where(j < 8, FAR, jnp.where(j < 16, 4, jnp.where(j < 32, 2, 1)))
    slope = jnp.where(j < 8, 0.125, jnp.where(j < 16, 0.25, jnp.where(j < 32, 0.5, 1.0)))
    row_key = jnp.left_shift(jnp.where(j < jnp.right_shift(cols, 2), row, 1 << 12), 8)
    past = 256 - reach + gap
    past = jnp.where(past == 256, 0, past)
    rows = pl.ds(pl.multiple_of(step * 32, 32), 32)
    for half in range(2):
        p = lax.broadcasted_iota(jnp.int32, (1, 128), 1) + 128 * half
        at = jnp.left_shift(p & (cols - 1), 8 - lx)
        key = jnp.left_shift(jnp.right_shift(p, lx), 8)
        other = key ^ row_key
        apart = (at - place) & 255
        delta = apart | other

        def pick(target, weight):
            return jnp.where(delta == target, weight, 0.0)

        here, right, left = delta == 0, delta == reach, delta == 256 - reach
        tree = jnp.where(here, 1.0, 0.0) - jnp.where(right, 0.5, 0.0) - jnp.where(left, 0.5, 0.0)
        full = (
            centre * tree
            + behind * (pick(256 - gap, 1.0) - pick(reach - gap, 0.5) - pick(256 - reach - gap, 0.5))
            + ahead * (pick(gap, 1.0) - pick(reach + gap, 0.5) - pick(past, 0.5))
        )
        high, low = split(full)
        quart = (TAU * tree).astype(jnp.bfloat16)
        for slot, table in enumerate((high, high, low, quart, quart)):
            left_ref[grid, rows, slot * 256 + half * 128 : slot * 256 + half * 128 + 128] = table
        near = jnp.minimum(apart, 256 - apart).astype(jnp.float32)
        hat = jnp.where(other == 0, jnp.maximum(0.0, 1.0 - near * slope), 0.0).astype(jnp.bfloat16)
        lanes = slice(half * 128, half * 128 + 128)
        hat_ref[grid, rows, lanes] = hat
        hat_ref[grid, pl.ds(pl.multiple_of(256 + step * 32, 32), 32), lanes] = hat


def class_weights(grid, lv_ref, vel_ref):
    m = lv_ref[grid, 1] - 5
    rows = jnp.left_shift(1, m).astype(jnp.float32)
    weights = stencil(vel_ref[grid, 1] * rows * 0.125)
    return [[jnp.where(m == c, w, 0.0) for w in weights] for c in range(4)]


class Sums:
    def __init__(self):
        self.held = {}

    def add(self, offset, number, value):
        key = (offset, number)
        self.held[key] = value if key not in self.held else self.held[key] + value


def spread(blocks, weights, own, up, down):
    for c in range(4):
        centre, behind, ahead = weights[c]
        count = 1 << c
        per = 8 >> c
        for n in range(per):
            w = [blocks[k * per + n] for k in range(count)]
            moved = []
            for k in range(count):
                value = centre * w[k]
                if k > 0:
                    value += behind * w[k - 1]
                if k < count - 1:
                    value += ahead * w[k + 1]
                moved.append(value)
            above, below = behind * w[-1], ahead * w[0]
            line = moved + [above]
            own.add(0, n, moved[0])
            up.add(0, n, above)
            if count == 1:
                down.add(0, n, below)
            for k in range(1, count):
                s = k & -k
                own.add(k * 8 // count, n, line[k] - 0.5 * (line[k - s] + line[k + s]))
            level = 2
            while level <= count:
                up.add(8 // level, n, -0.5 * above)
                spill = -0.5 * moved[0]
                if level == count:
                    spill += below
                down.add(8 - 8 // level, n, spill)
                level *= 2


def own_row(low):
    return 360 + low if low < 24 else 96 + low if low < 144 else 240 + low


def contribute(first, weights_row, blocks_ref, at, sums_ref):
    own, up, down = Sums(), Sums(), Sums()
    for grid in range(2):
        blocks = [blocks_ref[at, grid, 8 * n : 8 * n + 8, :] for n in range(8)]
        spread(blocks, weights_of(weights_row, grid), own, up, down)
    for offset, (start, count) in BLOCKS.items():
        for n in range(count):
            low = 8 * (start + n)
            targets = [(own_row(low), own)]
            if offset in UP:
                targets.append((240 + low - UP_ROWS[0], up))
            if offset in DOWN:
                targets.append((low - DOWN_ROWS[0], down))
            for row, sums in targets:
                value = sums.held[offset, n]
                sums_ref[row : row + 8, :] = value if first else sums_ref[row : row + 8, :] + value


def weights_of(row, grid):
    return [
        [jnp.broadcast_to(row[:, 12 * grid + 3 * c + n : 12 * grid + 3 * c + n + 1], (8, 128)) for n in range(3)]
        for c in range(4)
    ]


def make_nodes(sums_ref, halo, node_ref, next_ref, back_ref):
    after_in, before_in, up_far, down_far = halo

    def block(ref, n, start=0):
        return ref[start + 8 * n : start + 8 * n + 8, :]

    def held(offset, n):
        at = BLOCKS[offset][0] + n
        value = block(sums_ref, 0, own_row(8 * at))
        if offset in UP:
            value += block(after_in, at, 120)
        if offset in DOWN:
            value += block(before_in, at - 3)
        return value

    def before(offset, n):
        at = BLOCKS[offset][0] + n - 3
        value = block(after_in, at) + block(sums_ref, at)
        return value + block(up_far, at) if offset in (0, 4) else value

    for n in range(8):
        node = {0: held(0, n), 8: block(before_in, n, 120) + block(sums_ref, 3 + n, 240) + block(down_far, n)}
        last = before(0, n)
        back_ref[0, n] = last
        next_ref[n] = node[8]
        node_ref[0, n] = node[0]
        for c in range(1, 4):
            if n >= 8 >> c:
                break
            s = 8 >> c
            for k in range(1, 1 << c, 2):
                node[k * s] = held(k * s, n) + 0.5 * (node[k * s - s] + node[k * s + s])
                node_ref[k * s, n] = node[k * s]
            last = before(8 - s, n) + 0.5 * (last + node[0])
            back_ref[c, n] = last


def interpolate(weights_row, node_ref, next_ref, back_ref, g_ref, at):
    weights = [weights_of(weights_row, grid) for grid in range(2)]
    sums = [Sums(), Sums()]
    for c in range(4):
        per = 8 >> c
        count = 1 << c
        for n in range(per):
            line = [back_ref[c, n]] + [node_ref[k * per, n] for k in range(count)] + [next_ref[n]]
            for k in range(count):
                for grid in range(2):
                    centre, behind, ahead = weights[grid][c]
                    sums[grid].add(
                        0, k * per + n, centre * line[k + 1] + behind * line[k] + ahead * line[k + 2]
                    )
    for grid in range(2):
        for n in range(8):
            g_ref[at, grid, 8 * n : 8 * n + 8, :] = sums[grid].held[0, n]


def kernel(
    nz, nd,
    lv_hbm, vel_hbm, rate_hbm, coef_hbm, v_hbm, s_hbm, out_ref,
    lv_ref, vel_ref, rate_ref, coef_ref, v_ref, s_ref, left_ref, right_ref, hat_ref,
    w_ref, w_in, row_ref, row_in, sums_ref,
    after_in, before_in, up_far, down_far,
    node_ref, next_ref, back_ref, g_ref, g_in,
    small_sem, load_sem, w_sem, row_sem, halo_sem, g_sem,
):
    z, d = lax.axis_index("grid"), lax.axis_index("dom")
    small = [
        pltpu.make_async_copy(source, target, small_sem.at[n])
        for n, (source, target) in enumerate(
            ((lv_hbm, lv_ref), (vel_hbm, vel_ref), (rate_hbm, rate_ref), (coef_hbm, coef_ref))
        )
    ]
    for copy in small:
        copy.start()
    loads = []
    for grid in range(2):
        for n, (source, target) in enumerate(((v_hbm, v_ref), (s_hbm, s_ref))):
            loads.append(pltpu.make_async_copy(source.at[grid], target.at[grid], load_sem.at[grid, n]))
            loads[-1].start()

    barrier = pltpu.get_barrier_semaphore()
    peers = [(lax.rem(z + n, nz), d) for n in range(1, nz)]
    peers += [(z, lax.rem(d + n, nd)) for n in (1, 2, nd - 1, nd - 2)]
    for peer in peers:
        pl.semaphore_signal(barrier, inc=1, device_id=peer, device_id_type=MESH)

    def remote(source, target, send, recv, peer):
        return pltpu.make_async_remote_copy(
            src_ref=source, dst_ref=target, send_sem=send, recv_sem=recv, device_id=peer, device_id_type=MESH
        )

    def near_first(i):
        return lax.rem(z + jnp.where((i + d) % 2 == 0, 1 + i // 2, nz - 1 - i // 2), nz)

    for copy in small:
        copy.wait()
    lane = lax.broadcasted_iota(jnp.int32, (1, 128), 1)
    row = jnp.zeros((1, 128), jnp.float32)
    for grid in range(2):
        for c, weights in enumerate(class_weights(grid, lv_ref, vel_ref)):
            for n, weight in enumerate(weights):
                row = jnp.where(lane == 12 * grid + 3 * c + n, weight, row)
    row_ref[...] = row
    for grid in range(2):
        @pl.loop(0, 8)
        def _(step):
            build_tables(grid, step, lv_ref, vel_ref, rate_ref, left_ref, hat_ref)

    for grid in range(2):
        loads[2 * grid].wait()
        loads[2 * grid + 1].wait()
        vh, vl = split(v_ref[grid])
        sh, sl = split(s_ref[grid])
        for slot, part in enumerate((vh, vl, vh, sh, sl)):
            right_ref[grid, :, slot * 256 : slot * 256 + 256] = part
        w = dot(left_ref[grid], right_ref[grid], ((1,), (1,))) * coef_ref[grid].astype(jnp.float32)
        for half in range(2):
            for quarter in range(QUARTERS):
                w_ref[half * QUARTERS + quarter, grid] = w[
                    quarter * 64 : quarter * 64 + 64, half * 128 : half * 128 + 128
                ]

    pl.semaphore_wait(barrier, len(peers))

    def w_copy(slot, target, peer):
        return remote(w_ref.at[peer], w_in.at[slot], w_sem.at[0, peer], w_sem.at[1, slot], (target, d))

    def row_copy(slot, target, peer):
        return remote(row_ref, row_in.at[slot], row_sem.at[0, peer], row_sem.at[1, slot], (target, d))

    @pl.loop(0, nz - 1)
    def _(i):
        peer = near_first(i)
        row_copy(z, peer, peer).start()
        w_copy(z, peer, peer).start()

    contribute(True, row_ref[...], w_ref, z, sums_ref)

    @pl.loop(0, nz - 1)
    def _(i):
        peer = near_first(i)
        row_copy(peer, peer, peer).wait_recv()
        w_copy(peer, peer, peer).wait_recv()
        contribute(False, row_in[peer], w_in, peer, sums_ref)

    def halo_copy(n, source, target, step):
        return remote(source, target, halo_sem.at[0, n], halo_sem.at[1, n], (z, lax.rem(d + nd + step, nd)))

    halos = [
        halo_copy(0, sums_ref.at[264:360, :], up_far, 2),
        halo_copy(1, sums_ref.at[0:64, :], down_far, -2),
        halo_copy(2, sums_ref.at[120:360, :], after_in, 1),
        halo_copy(3, sums_ref.at[0:184, :], before_in, -1),
    ]
    for copy in halos:
        copy.start()
    for copy in halos:
        copy.wait_recv()
    make_nodes(
        sums_ref, (after_in, before_in, up_far, down_far), node_ref, next_ref, back_ref,
    )

    def g_copy(slot, target, peer):
        return remote(g_ref.at[peer], g_in.at[slot], g_sem.at[0, peer], g_sem.at[1, slot], (target, d))

    @pl.loop(0, nz)
    def _(i):
        peer = jnp.where(i < 3, lax.rem(i + 2, 3), jnp.where(i == 5, 6, jnp.where(i == 6, 5, i)))

        @pl.when(peer != z)
        def _():
            interpolate(row_in[peer], node_ref, next_ref, back_ref, g_ref, peer)
            g_copy(z, peer, peer).start()

    interpolate(row_ref[...], node_ref, next_ref, back_ref, g_in, z)

    for half in range(2):
        @pl.loop(half * QUARTERS, half * QUARTERS + QUARTERS)
        def _(peer):
            @pl.when(peer != z)
            def _():
                g_copy(peer, peer, peer).wait_recv()

        for grid in range(2):
            turned = jnp.transpose(
                jnp.concatenate([g_in[half * QUARTERS + n, grid] for n in range(QUARTERS)], axis=0)
            )
            high, low = split(turned)
            lanes = jnp.concatenate([high, low], axis=1)
            rows = slice(half * 128, half * 128 + 128)
            out_ref[grid, rows, :] = dot(lanes, hat_ref[grid], ((1,), (0,)))

    for copy in halos:
        copy.wait_send()

    @pl.loop(0, nz - 1)
    def _(i):
        peer = near_first(i)
        row_copy(z, peer, peer).wait_send()
        w_copy(z, peer, peer).wait_send()
        g_copy(z, peer, peer).wait_send()


def local(nz, nd, nodal_values, source_term, velocity, react_rate, levels, comb_coefs):
    f32, bf16 = jnp.float32, jnp.bfloat16
    hbm = pl.BlockSpec(memory_space=pl.ANY)
    sem = pltpu.SemaphoreType.DMA
    return pl.pallas_call(
        functools.partial(kernel, nz, nd),
        out_shape=jax.ShapeDtypeStruct((2, 256, 256), f32),
        in_specs=[hbm] * 6,
        out_specs=pl.BlockSpec(memory_space=pltpu.VMEM),
        scratch_shapes=[
            pltpu.SMEM((2, 2), jnp.int32),
            pltpu.SMEM((2, 2), f32),
            pltpu.SMEM((2,), f32),
            pltpu.SMEM((2,), jnp.int32),
            pltpu.VMEM((2, 256, 256), f32),
            pltpu.VMEM((2, 256, 256), f32),
            pltpu.VMEM((2, 256, KDIM), bf16),
            pltpu.VMEM((2, 256, KDIM), bf16),
            pltpu.VMEM((2, 512, 256), bf16),
            pltpu.VMEM((nz, 2, 64, 128), f32),
            pltpu.VMEM((nz, 2, 64, 128), f32),
            pltpu.VMEM((1, 128), f32),
            pltpu.VMEM((nz, 1, 128), f32),
            pltpu.VMEM((SUM_ROWS, 128), f32),
            pltpu.VMEM((240, 128), f32),
            pltpu.VMEM((184, 128), f32),
            pltpu.VMEM((96, 128), f32),
            pltpu.VMEM((64, 128), f32),
            pltpu.VMEM((8, 8, 8, 128), f32),
            pltpu.VMEM((8, 8, 128), f32),
            pltpu.VMEM((4, 8, 8, 128), f32),
            pltpu.VMEM((nz, 2, 64, 128), f32),
            pltpu.VMEM((nz, 2, 64, 128), f32),
            sem((4,)),
            sem((2, 2)),
            sem((2, nz)),
            sem((2, nz)),
            sem((2, 4)),
            sem((2, nz)),
        ],
        compiler_params=pltpu.CompilerParams(collective_id=0, has_side_effects=True, vmem_limit_bytes=40 << 20),
    )(*[pltpu.with_memory_space_constraint(x, pltpu.HBM) for x in (levels, velocity, react_rate, comb_coefs, nodal_values, source_term)])


def solution(mesh):
    in_specs = (
        P("grid", None, "dom"),
        P("grid", None, "dom"),
        P("grid", None),
        P("grid"),
        P("grid", None),
        P("grid"),
    )
    body = functools.partial(local, mesh.shape["grid"], mesh.shape["dom"])
    return jax.shard_map(body, mesh=mesh, in_specs=in_specs, out_specs=P("grid", None, "dom"), check_vma=False)
```
